256 devices in a mesh: gx: 128 (over y, z_lo, x, core), gy: 2 (over z_hi).
Axes of the slice: x: 4, y: 4, z: 8 (z_hi: 2, z_lo: 4; z = z_hi * 4 + z_lo), core: 2. Of those that a mesh axis runs over, the one named last changes fastest.
Arguments:
- coefficients: float32 [2, 16, 256, 256], P(None, None, 'gx'), may hold values from -6 to 6
- first_axis_basis: float32 [4096, 256], replicated, may hold values from -0.375 to 0.375
- basis_y: float32 [256, 256], P('gy'), may hold values from -0.375 to 0.375
- basis_z: float32 [32, 16], replicated, may hold values from -1.5 to 1.5
- conductivity: float32 [32, 4096, 256], P(None, 'gx', 'gy'), may hold values from 0.3 to 3
- pressure: float32 [32, 4096, 256], P(None, 'gx', 'gy'), may hold values from -6 to 6
Outputs:
- hess_action: float32 [2, 16, 256, 256], P(None, None, 'gx', 'gy')
The draws below stay inside these ranges and needn't reach their ends.
All inputs are finite; a program needn't handle non-finite values.
Results may differ from the reference program's by a relative error of at most 0.000067.
Values sent between devices are 32-bit elements; how exact they have to be, the bound alone decides.
No kernel may reach another device: no remote copies, remote signals or barrier semaphores. Data moves between devices by JAX's collectives and lax.ppermute only.
A program may use at most 128 MiB of HBM per device.

```python
import math
import jax
import jax.numpy as jnp
from jax import lax

MX = 256
MY = 256
MZ = 16
NZ = 32
NX = 4096
NY = 256


def steps_of(stream_key, shape, shards, low, top_value):
    gain, own = 1.0, jax.random.fold_in(stream_key, 6)
    for position, shards_of in shards:
        heights = jnp.exp(jax.random.uniform(jax.random.fold_in(own, position), (shards_of,), jnp.float32, low / len(shards), top_value / len(shards)))
        gain = gain * jnp.repeat(heights, shape[position] // shards_of).reshape([-1 if axis == position else 1 for axis in range(len(shape))])
    return gain


def normal_values(key, shape, width, bound, pieces=(), held_as=jnp.bfloat16):
    array = jax.random.normal(key, shape, jnp.float32) * width
    if len(pieces) > 0:
        array = steps_of(key, shape, pieces, -0.22, 0.18) * array
    return jnp.clip(array, min=-bound, max=bound).astype(held_as)


def setup_inputs(seed: int = 0) -> dict:
    keys = jax.random.split(jax.random.key(seed), 7)
    return {
        "coefficients": normal_values(keys[0], (2, MZ, MX, MY), 1.0, 6.0, ((2, 128),), jnp.float32),
        "first_axis_basis": normal_values(keys[1], (NX, MX), MX ** -0.5, 0.375, (), jnp.float32),
        "basis_y": normal_values(keys[2], (NY, MY), MY ** -0.5, 0.375, ((0, 2),), jnp.float32),
        "basis_z": normal_values(keys[3], (NZ, MZ), MZ ** -0.5, 1.5, (), jnp.float32),
        "conductivity": jnp.clip(jnp.exp(math.log(3.0) - 2.3025851 * jax.random.uniform(keys[4], (NZ, NX, NY), jnp.float32) ** steps_of(keys[4], (NZ, NX, NY), ((1, 128), (2, 2)), -0.2, 0.2)), 0.3, 3.0),
        "pressure": normal_values(keys[5], (NZ, NX, NY), 1.0, 6.0, ((1, 128), (2, 2)), jnp.float32),
    }


step_size = 0.05
highest = lax.Precision.HIGHEST


def shifted(values, axis, side):
    length = values.shape[axis]
    widths = [(0, 0)] * values.ndim
    if side < 0:
        part = lax.slice_in_dim(values, 0, length - 1, axis=axis)
        widths[axis] = (1, 0)
    else:
        part = lax.slice_in_dim(values, 1, length, axis=axis)
        widths[axis] = (0, 1)
    return jnp.pad(part, widths)


def flow(coeffs, values):
    total = jnp.zeros(values.shape, jnp.float32)
    filled = jnp.ones(values.shape, jnp.float32)
    for axis in (1, 2, 0):
        for side in (-1, 1):
            valid = shifted(filled, axis, side)
            total = total + valid * (0.5 * (coeffs + shifted(coeffs, axis, side)) * (shifted(values, axis, side) - values))
    return total


def coupling(coeffs, values):
    total = jnp.zeros(values.shape, jnp.float32)
    filled = jnp.ones(values.shape, jnp.float32)
    for axis in (1, 2, 0):
        for side in (-1, 1):
            valid = shifted(filled, axis, side)
            total = total + valid * ((shifted(coeffs, axis, side) - coeffs) * (shifted(values, axis, side) - values))
    return total


def one_direction(block, first_axis_basis, basis_y, basis_z, conductivity, pressure):
    along_x = jnp.einsum('xa,cab->cxb', first_axis_basis, block, precision=highest)
    along_y = jnp.einsum('yb,cxb->cxy', basis_y, along_x, precision=highest)
    perturbation = jnp.einsum('zc,cxy->zxy', basis_z, along_y, precision=highest)
    increment_field = conductivity * perturbation
    source = flow(increment_field, pressure)
    first = step_size * source
    second = first + step_size * (flow(conductivity, first) + source)
    adjoint = second + step_size * flow(conductivity, second)
    combined = step_size * (adjoint + second)
    sensitivity = -0.5 * conductivity * coupling(pressure, combined)
    backward_depth = jnp.einsum('zc,zxy->cxy', basis_z, sensitivity, precision=highest)
    back_y = jnp.einsum('yb,cxy->cxb', basis_y, backward_depth, precision=highest)
    back_x = jnp.einsum('xa,cxb->cab', first_axis_basis, back_y, precision=highest)
    return back_x + block


def reference(coefficients, first_axis_basis, basis_y, basis_z, conductivity, pressure):
    def apply_one(block):
        return one_direction(block, first_axis_basis, basis_y, basis_z, conductivity, pressure)
    return lax.map(apply_one, coefficients)
```

```python
import jax
import jax.numpy as jnp
from jax import lax
from jax.experimental import pallas as pl
from jax.experimental.pallas import tpu as pltpu
from jax.sharding import Mesh, PartitionSpec as P

step_size = 0.05
highest = lax.Precision.HIGHEST
f32 = jnp.float32

AXES = ("y", "zl", "x", "core", "zh")
SIZES = (4, 4, 4, 2, 2)
GX = ("y", "zl", "x", "core")
PLANE = ("y", "x", "core")
RING = ("zl", "zh")

DIRECTIONS, MODES_Z, DEPTH = 2, 16, 32
ROWS, COLS = 32, 128
HALO = 4
EXT_ROWS = ROWS + 2 * HALO
EXT_COLS = 2 * COLS
STRIP = 8
GROUPS = EXT_ROWS // STRIP
MODES = 256
BLOCK = 8 * ROWS
VMEM = pl.BlockSpec(memory_space=pltpu.VMEM)
SMEM = pl.BlockSpec(memory_space=pltpu.SMEM)
ANY = pl.BlockSpec(memory_space=pl.ANY)


def params():
    return pltpu.CompilerParams(vmem_limit_bytes=48 * 1024 * 1024)


def pack_kernel(where, kap, prs, upper, lower, rows_out, strip_out):
    zh = where[1]
    lane = lax.broadcasted_iota(jnp.int32, (STRIP, COLS), 1)

    def body(z, carry):
        packed = jnp.zeros((STRIP, COLS), f32)
        for f, ref in enumerate((kap, prs)):
            beside = jnp.concatenate([upper[f, z], lower[f, z]], axis=0)
            rows_out[f, z] = beside
            for g in range(GROUPS):
                tile = ref[z, pl.ds(8 * g, 8)] if g < ROWS // 8 else beside
                first = f * EXT_ROWS + 8 * g
                shift = lax.rem(first + 8 * (1 - zh), COLS)
                moved = pltpu.roll(tile, shift, 1)
                packed = jnp.where((lane >= first) & (lane < first + 8), moved, packed)
        strip_out[z] = packed
        return carry

    lax.fori_loop(0, DEPTH, body, 0)


def pack(where, kap, prs, upper, lower):
    return pl.pallas_call(
        pack_kernel,
        out_shape=(
            jax.ShapeDtypeStruct((2, DEPTH, 2 * HALO, COLS), f32),
            jax.ShapeDtypeStruct((DEPTH, STRIP, COLS), f32),
        ),
        in_specs=[SMEM] + [VMEM] * 4,
        out_specs=(VMEM, VMEM),
        compiler_params=params(),
        cost_estimate=pl.CostEstimate(flops=2_000_000, bytes_accessed=1_600_000, transcendentals=0),
        name="pack",
    )(where, kap, prs, upper, lower)


def expand_kernel(where, coefs, basis, beside, first_basis, out, wide, blocks, sems):
    zl = where[2]
    copies = []
    for y in range(4):
        start = pl.multiple_of((y * 4 + zl) * BLOCK, BLOCK)
        below = pl.multiple_of(jnp.maximum(start - 8, 0), 8)
        above = pl.multiple_of(jnp.minimum(start + BLOCK, 4096 - 8), 8)
        for part, (src, size, dst) in enumerate(
            ((below, 8, 0), (start, BLOCK, 8), (above, 8, BLOCK + 8))
        ):
            copies.append(
                pltpu.make_async_copy(
                    first_basis.at[pl.ds(src, size)],
                    blocks.at[y, pl.ds(dst, size)],
                    sems.at[y, part],
                )
            )
    for copy in copies:
        copy.start()
    wide[pl.ds(0, COLS)] = basis[...]
    wide[pl.ds(COLS, STRIP)] = beside[...]
    wide[pl.ds(COLS + STRIP, COLS - STRIP)] = jnp.zeros((COLS - STRIP, MODES), f32)
    columns = lax.dot_general(
        coefs[...], wide[...], (((1,), (1,)), ((), ())),
        precision=highest, preferred_element_type=f32,
    )
    lane = lax.broadcasted_iota(jnp.int32, (STRIP, COLS), 1)
    low = lax.broadcasted_iota(jnp.int32, (STRIP, EXT_COLS), 0) < HALO
    for copy in copies:
        copy.wait()
    for y in range(4):
        full = lax.dot_general(
            blocks[y], columns, (((1,), (0,)), ((), ())),
            precision=highest, preferred_element_type=f32,
        )
        for k in range(8):
            own = full[8 + ROWS * k : 8 + ROWS * (k + 1)]
            above = full[8 + ROWS * (k + 1) : 16 + ROWS * (k + 1)]
            below = full[ROWS * k : ROWS * k + 8]
            ends = jnp.where(low, above, below)
            q = y * 8 + k
            out[q, pl.ds(0, ROWS)] = own[:, :COLS]
            out[q, pl.ds(ROWS, 8)] = ends[:, :COLS]
            packed = own[:8, COLS:]
            for g in range(1, GROUPS):
                tile = (own[8 * g : 8 * g + 8] if g < ROWS // 8 else ends)[:, COLS:]
                packed = jnp.where(lane < 8 * g, packed, pltpu.roll(tile, 8 * g, 1))
            out[q, pl.ds(EXT_ROWS, STRIP)] = packed


def expand(where, coefs, basis, beside, first_basis):
    return pl.pallas_call(
        expand_kernel,
        out_shape=jax.ShapeDtypeStruct((32, EXT_ROWS + STRIP, COLS), f32),
        in_specs=[SMEM, VMEM, VMEM, VMEM, ANY],
        out_specs=VMEM,
        scratch_shapes=[
            pltpu.VMEM((EXT_COLS, MODES), f32),
            pltpu.VMEM((4, BLOCK + 16, MODES), f32),
            pltpu.SemaphoreType.DMA((4, 3)),
        ],
        compiler_params=params(),
        cost_estimate=pl.CostEstimate(
            flops=6 * 2 * 256 * 256 * 1344, bytes_accessed=3_000_000, transcendentals=0
        ),
        name="expand",
    )(where, coefs, basis, beside, first_basis)


def grid_kernel(
    where, basis_z, layers, kap, prs, rows, strip, out,
    kk, pp, ex, ey, ez, px, py, pz, field, sens,
):
    gx, zh = where[0], where[1]
    row = lax.broadcasted_iota(jnp.int32, (EXT_ROWS, EXT_COLS), 0)
    col = lax.broadcasted_iota(jnp.int32, (EXT_ROWS, EXT_COLS), 1)
    no_x = ((row == ROWS - 1) & (gx == 127)) | ((row == EXT_ROWS - 1) & (gx == 0))
    no_y = ((col == COLS - 1) & (zh == 1)) | ((col == EXT_COLS - 1) & (zh == 0))
    mask_x = jnp.where(no_x, 0.0, 1.0).astype(f32)
    mask_y = jnp.where(no_y, 0.0, 1.0).astype(f32)
    core = pl.ds(0, COLS)
    side = pl.ds(COLS, COLS)

    def shift_of(lane):
        return lax.rem(120 * zh + 2 * COLS - lane, COLS)

    def x_next(v):
        return pltpu.roll(v, EXT_ROWS - 1, 0)

    def x_prev(v):
        return pltpu.roll(v, 1, 0)

    def y_next(v):
        return pltpu.roll(v, EXT_COLS - 1, 1)

    def y_prev(v):
        return pltpu.roll(v, 1, 1)

    def place(z, carry):
        for f, (src, dst) in enumerate(((kap, kk), (prs, pp))):
            dst[z, pl.ds(0, ROWS), core] = src[z]
            dst[z, pl.ds(ROWS, 8), core] = rows[f, z]
            packed = strip[z]
            for g in range(GROUPS):
                dst[z, pl.ds(8 * g, 8), side] = pltpu.roll(
                    packed, shift_of(f * EXT_ROWS + 8 * g), 1
                )
        return carry

    lax.fori_loop(0, DEPTH, place, 0)

    half = 0.5 * step_size * step_size

    def edges(z, carry):
        later = jnp.minimum(z + 1, DEPTH - 1)
        inside = jnp.where(z < DEPTH - 1, 1.0, 0.0).astype(f32)
        k, p = kk[z], pp[z]
        ex[z] = (half * mask_x) * (k + x_next(k))
        ey[z] = (half * mask_y) * (k + y_next(k))
        ez[z] = (half * inside) * (k + kk[later])
        px[z] = (0.5 * mask_x) * (x_next(p) - p)
        py[z] = (0.5 * mask_y) * (y_next(p) - p)
        pz[z] = (0.5 * inside) * (pp[later] - p)
        return carry

    lax.fori_loop(0, DEPTH, edges, 0)

    def layers_of(z, carry):
        for d in range(DIRECTIONS):
            total = basis_z[z, 0] * layers[d * MODES_Z]
            for c in range(1, MODES_Z):
                total = total + basis_z[z, c] * layers[d * MODES_Z + c]
            field[d, z, :, core] = kk[z, :, core] * total[:EXT_ROWS]
            packed = total[EXT_ROWS:]
            for g in range(GROUPS):
                at = pl.ds(8 * g, 8)
                field[d, z, at, side] = kk[z, at, side] * pltpu.roll(packed, shift_of(8 * g), 1)
        return carry

    lax.fori_loop(0, DEPTH, layers_of, 0)

    nothing = tuple(jnp.zeros((EXT_ROWS, EXT_COLS), f32) for _ in range(DIRECTIONS))

    def source_of(z, before):
        later = jnp.minimum(z + 1, DEPTH - 1)
        after = []
        for d in range(DIRECTIONS):
            c = field[d, z]
            fx = (c + x_next(c)) * px[z]
            fy = (c + y_next(c)) * py[z]
            fz = (c + field[d, later]) * pz[z]
            field[d, z] = (fx - x_prev(fx)) + (fy - y_prev(fy)) + (fz - before[d])
            after.append(fz)
        return tuple(after)

    lax.fori_loop(0, DEPTH, source_of, nothing)

    def advance(z, before):
        later = jnp.minimum(z + 1, DEPTH - 1)
        after = []
        for d in range(DIRECTIONS):
            u = field[d, z]
            fx = (x_next(u) - u) * ex[z]
            fy = (y_next(u) - u) * ey[z]
            fz = (field[d, later] - u) * ez[z]
            field[d, z] = (
                (2.0 * step_size) * u + (fx - x_prev(fx)) + (fy - y_prev(fy)) + (fz - before[d])
            )
            after.append(fz)
        return tuple(after)

    lax.fori_loop(0, DEPTH, advance, nothing)
    lax.fori_loop(0, DEPTH, advance, nothing)

    def couple(z, before):
        later = jnp.minimum(z + 1, DEPTH - 1)
        after = []
        for d in range(DIRECTIONS):
            w = field[d, z]
            fx = (x_next(w) - w) * px[z]
            fy = (y_next(w) - w) * py[z]
            fz = (field[d, later] - w) * pz[z]
            total = (fx + x_prev(fx)) + (fy + y_prev(fy)) + (fz + before[d])
            sens[d, z] = -kap[z] * total[:ROWS, :COLS]
            after.append(fz)
        return tuple(after)

    lax.fori_loop(0, DEPTH, couple, nothing)

    def modes_of(c, carry):
        for d in range(DIRECTIONS):
            total = basis_z[0, c] * sens[d, 0]
            for z in range(1, DEPTH):
                total = total + basis_z[z, c] * sens[d, z]
            out[d * MODES_Z + c] = total
        return carry

    lax.fori_loop(0, MODES_Z, modes_of, 0)


def on_grid(where, basis_z, layers, kap, prs, rows, strip):
    wide = (DEPTH, EXT_ROWS, EXT_COLS)
    return pl.pallas_call(
        grid_kernel,
        out_shape=jax.ShapeDtypeStruct((DIRECTIONS * MODES_Z, ROWS, COLS), f32),
        in_specs=[SMEM, SMEM] + [VMEM] * 5,
        out_specs=VMEM,
        scratch_shapes=[pltpu.VMEM(wide, f32) for _ in range(8)]
        + [
            pltpu.VMEM((DIRECTIONS,) + wide, f32),
            pltpu.VMEM((DIRECTIONS, DEPTH, ROWS, COLS), f32),
        ],
        compiler_params=params(),
        cost_estimate=pl.CostEstimate(
            flops=100_000_000, bytes_accessed=3_000_000, transcendentals=0
        ),
        name="on_grid",
    )(where, basis_z, layers, kap, prs, rows, strip)


def project_kernel(where, values, basis, first_basis, out, blocks, sems):
    zl = where[2]
    copies = []
    for y in range(4):
        start = pl.multiple_of((y * 4 + zl) * BLOCK, BLOCK)
        copies.append(
            pltpu.make_async_copy(
                first_basis.at[pl.ds(start, BLOCK)], blocks.at[pl.ds(y * BLOCK, BLOCK)], sems.at[y]
            )
        )
    for copy in copies:
        copy.start()
    for copy in copies:
        copy.wait()
    along_x = lax.dot_general(
        blocks[...], values[...], (((0,), (0,)), ((), ())),
        precision=highest, preferred_element_type=f32,
    )
    full = lax.dot_general(
        along_x, basis[...], (((1,), (0,)), ((), ())),
        precision=highest, preferred_element_type=f32,
    )
    for y in range(4):
        for z in range(4):
            at = y * 64 + z * 16
            for h in range(2):
                out[z * 2 + h, pl.ds(y * 16, 16)] = full[at : at + 16, h * 128 : (h + 1) * 128]


def project(where, values, basis, first_basis):
    return pl.pallas_call(
        project_kernel,
        out_shape=jax.ShapeDtypeStruct((8, 64, 128), f32),
        in_specs=[SMEM, VMEM, VMEM, ANY],
        out_specs=VMEM,
        scratch_shapes=[
            pltpu.VMEM((4 * BLOCK, MODES), f32),
            pltpu.SemaphoreType.DMA((4,)),
        ],
        compiler_params=params(),
        cost_estimate=pl.CostEstimate(
            flops=6 * 2 * 256 * 128 * 1280, bytes_accessed=2_000_000, transcendentals=0
        ),
        name="project",
    )(where, values, basis, first_basis)


def exchanged(values, axes):
    return lax.all_to_all(values, axes, split_axis=0, concat_axis=0, tiled=True)


def per_device(coefficients, first_axis_basis, basis_y, basis_z, conductivity, pressure):
    gx = lax.axis_index(GX)
    zh = lax.axis_index("zh")
    where = jnp.stack([gx, zh, lax.axis_index("zl")]).astype(jnp.int32)
    swap = [(0, 1), (1, 0)]

    flat = coefficients.reshape(DIRECTIONS * MODES_Z, 2, MODES)
    spread = jnp.broadcast_to(flat.reshape(4, 1, 8, 2, MODES), (4, 4, 8, 2, MODES))
    gathered = exchanged(spread.reshape(128, 2, MODES), GX)

    beside = lax.ppermute(
        lax.dynamic_slice_in_dim(basis_y, (COLS - STRIP) * (1 - zh), STRIP, 0), "zh", swap
    )
    statics = jnp.stack([conductivity, pressure])
    upper = lax.ppermute(statics[:, :, :HALO], GX, [((i + 1) % 128, i) for i in range(128)])
    lower = lax.ppermute(statics[:, :, -HALO:], GX, [(i, (i + 1) % 128) for i in range(128)])
    rows, strip = pack(where, conductivity, pressure, upper, lower)
    strip = lax.ppermute(strip, "zh", swap)

    message = expand(where, gathered.reshape(MODES, MODES), basis_y, beside, first_axis_basis)
    layers = exchanged(message, PLANE)
    modes = on_grid(where, basis_z, layers, conductivity, pressure, rows, strip)
    columns = exchanged(modes, PLANE)
    shares = project(where, columns.reshape(4 * BLOCK, COLS), basis_y, first_axis_basis)
    summed = jnp.sum(exchanged(shares, RING), axis=0)
    result = exchanged(summed.reshape(32, 2, 128), PLANE)
    own = lax.dynamic_slice_in_dim(coefficients, zh * 128, 128, 3)
    return result.reshape(DIRECTIONS, MODES_Z, 2, 128) + own


def solution(mesh):
    split = Mesh(mesh.devices.reshape(SIZES), AXES)
    return jax.shard_map(
        per_device,
        mesh=split,
        in_specs=(
            P(None, None, GX, None),
            P(),
            P("zh", None),
            P(),
            P(None, GX, "zh"),
            P(None, GX, "zh"),
        ),
        out_specs=P(None, None, GX, "zh"),
        check_vma=False,
    )
```

```python
import jax
import jax.numpy as jnp
from jax import lax
from jax.experimental import pallas as pl
from jax.experimental.pallas import tpu as pltpu
from jax.sharding import Mesh, PartitionSpec as P

step_size = 0.05
highest = lax.Precision.HIGHEST
f32 = jnp.float32

AXES = ("y", "zl", "x", "core", "zh")
SIZES = (4, 4, 4, 2, 2)
GX = ("y", "zl", "x", "core")
PLANE = ("y", "x", "core")
RING = ("zl", "zh")

DIRECTIONS, MODES_Z, DEPTH = 2, 16, 32
ROWS, COLS = 32, 128
HALO = 4
EXT_ROWS = ROWS + 2 * HALO
EXT_COLS = 2 * COLS
STRIP = 8
GROUPS = EXT_ROWS // STRIP
PER_STEP = 16
LAYER_STEP = 4
STATIC_STEP = 8
MODES = 256
FIELDS = 14
BLOCK = 8 * ROWS
VMEM = pl.BlockSpec(memory_space=pltpu.VMEM)
SMEM = pl.BlockSpec(memory_space=pltpu.SMEM)
HBM = pl.BlockSpec(memory_space=pltpu.HBM)


def params(mib):
    return pltpu.CompilerParams(vmem_limit_bytes=mib * 1024 * 1024)


def strip_shift(zh, lane):
    return lax.rem(120 * zh + 2 * COLS - lane, COLS)


def columns_on(c, h, last):
    c, h = pltpu.roll(c, COLS - 1, 1), pltpu.roll(h, COLS - 1, 1)
    return jnp.where(last, h, c), jnp.where(last, c, h)


def pack_kernel(where, kap, prs, upper, lower, rows_out, strip_out):
    zh = where[1]
    lane = lax.broadcasted_iota(jnp.int32, (STRIP, COLS), 1)

    def body(i, carry):
        for j in range(LAYER_STEP):
            z = i * LAYER_STEP + j
            packed = jnp.zeros((STRIP, COLS), f32)
            for f, ref in enumerate((kap, prs)):
                beside = jnp.concatenate([upper[f, z], lower[f, z]], axis=0)
                rows_out[f, z] = beside
                for g in range(GROUPS):
                    tile = ref[z, pl.ds(8 * g, 8)] if g < ROWS // 8 else beside
                    first = f * EXT_ROWS + 8 * g
                    moved = pltpu.roll(tile, lax.rem(first + 8 * (1 - zh), COLS), 1)
                    packed = jnp.where((lane >= first) & (lane < first + 8), moved, packed)
            strip_out[z] = packed
        return carry

    lax.fori_loop(0, DEPTH // LAYER_STEP, body, 0)


def pack(where, kap, prs, upper, lower):
    return pl.pallas_call(
        pack_kernel,
        out_shape=(
            jax.ShapeDtypeStruct((2, DEPTH, 2 * HALO, COLS), f32),
            jax.ShapeDtypeStruct((DEPTH, STRIP, COLS), f32),
        ),
        in_specs=[SMEM] + [VMEM] * 4,
        out_specs=(VMEM, VMEM),
        compiler_params=params(52),
        cost_estimate=pl.CostEstimate(flops=2_000_000, bytes_accessed=1_600_000, transcendentals=0),
        name="pack",
    )(where, kap, prs, upper, lower)


def expand_kernel(where, coefs, basis, beside, first_basis, out, wide, blocks, sems):
    zl = where[2]
    copies = []
    for y in range(4):
        start = pl.multiple_of((y * 4 + zl) * BLOCK, BLOCK)
        below = pl.multiple_of(jnp.maximum(start - 8, 0), 8)
        above = pl.multiple_of(jnp.minimum(start + BLOCK, 4096 - 8), 8)
        for part, (src, size, dst) in enumerate(
            ((below, 8, 0), (start, BLOCK, 8), (above, 8, BLOCK + 8))
        ):
            copies.append(
                pltpu.make_async_copy(
                    first_basis.at[pl.ds(src, size)],
                    blocks.at[y, pl.ds(dst, size)],
                    sems.at[y, part],
                )
            )
    for copy in copies:
        copy.start()
    wide[pl.ds(0, COLS)] = basis[...]
    wide[pl.ds(COLS, STRIP)] = beside[...]
    wide[pl.ds(COLS + STRIP, COLS - STRIP)] = jnp.zeros((COLS - STRIP, MODES), f32)
    columns = lax.dot_general(
        coefs[...], wide[...], (((1,), (1,)), ((), ())),
        precision=highest, preferred_element_type=f32,
    )
    lane = lax.broadcasted_iota(jnp.int32, (STRIP, COLS), 1)
    low = lax.broadcasted_iota(jnp.int32, (STRIP, EXT_COLS), 0) < HALO
    for copy in copies:
        copy.wait()
    for y in range(4):
        full = lax.dot_general(
            blocks[y], columns, (((1,), (0,)), ((), ())),
            precision=highest, preferred_element_type=f32,
        )
        for k in range(8):
            own = full[8 + ROWS * k : 8 + ROWS * (k + 1)]
            above = full[8 + ROWS * (k + 1) : 16 + ROWS * (k + 1)]
            below = full[ROWS * k : ROWS * k + 8]
            ends = jnp.where(low, above, below)
            q = y * 8 + k
            out[q, pl.ds(0, ROWS)] = own[:, :COLS]
            out[q, pl.ds(ROWS, 8)] = ends[:, :COLS]
            packed = own[:8, COLS:]
            for g in range(1, GROUPS):
                tile = (own[8 * g : 8 * g + 8] if g < ROWS // 8 else ends)[:, COLS:]
                packed = jnp.where(lane < 8 * g, packed, pltpu.roll(tile, 8 * g, 1))
            out[q, pl.ds(EXT_ROWS, STRIP)] = packed


def expand(where, coefs, basis, beside, first_basis):
    return pl.pallas_call(
        expand_kernel,
        out_shape=jax.ShapeDtypeStruct((32, EXT_ROWS + STRIP, COLS), f32),
        in_specs=[SMEM, VMEM, VMEM, VMEM, HBM],
        out_specs=VMEM,
        scratch_shapes=[
            pltpu.VMEM((EXT_COLS, MODES), f32),
            pltpu.VMEM((4, BLOCK + 16, MODES), f32),
            pltpu.SemaphoreType.DMA((4, 3)),
        ],
        compiler_params=params(52),
        cost_estimate=pl.CostEstimate(
            flops=6 * 2 * 256 * 256 * 1344, bytes_accessed=3_000_000, transcendentals=0
        ),
        name="expand",
    )(where, coefs, basis, beside, first_basis)


def statics_kernel(where, kap, prs, rows, strip, out, built, pp, ph, sem):
    kk, kh, pxc, pxh, pyc, pyh, pzc, pzh, exc, exh, eyc, eyh, ezc, ezh = (
        built.at[n] for n in range(FIELDS)
    )
    gx, zh = where[0], where[1]
    half = 0.5 * step_size * step_size

    def place(i, carry):
        for j in range(STATIC_STEP):
            z = i * STATIC_STEP + j
            packed = strip[z]
            for f, (src, dst, far) in enumerate(((kap, kk, kh), (prs, pp, ph))):
                ends = rows[f, z]
                dst[z, pl.ds(HALO, ROWS)] = src[z]
                dst[z, pl.ds(0, HALO)] = ends[HALO:]
                dst[z, pl.ds(HALO + ROWS, HALO)] = ends[:HALO]
                for g in range(GROUPS):
                    tile = pltpu.roll(packed, strip_shift(zh, f * EXT_ROWS + 8 * g), 1)
                    if g < ROWS // 8:
                        far[z, pl.ds(HALO + 8 * g, 8)] = tile
                    else:
                        far[z, pl.ds(0, HALO)] = tile[HALO:]
                        far[z, pl.ds(HALO + ROWS, HALO)] = tile[:HALO]
        return carry

    lax.fori_loop(0, DEPTH // STATIC_STEP, place, 0)

    lane = lax.broadcasted_iota(jnp.int32, (8, COLS), 1)
    row = lax.broadcasted_iota(jnp.int32, (8, COLS), 0)
    last = lane == COLS - 1
    mask_c = jnp.where(last & (zh == 1), 0.0, 1.0).astype(f32)
    mask_h = jnp.where(last & (zh == 0), 0.0, 1.0).astype(f32)
    lowest, highest_row = jnp.where(gx == 0, HALO - 1, -1), jnp.where(gx == 127, HALO + ROWS - 1, -1)

    for start in (0, 8, 16, 24, 31):
        at, up = pl.ds(start, 8), pl.ds(start + 1, 8)
        here = row + start
        mask_x = jnp.where((here == lowest) | (here == highest_row), 0.0, 1.0).astype(f32)

        def along_x(i, carry, at=at, up=up, mask_x=mask_x):
            for j in range(STATIC_STEP):
                z = i * STATIC_STEP + j
                exc[z, at] = (half * mask_x) * (kk[z, at] + kk[z, up])
                exh[z, at] = (half * mask_x) * (kh[z, at] + kh[z, up])
                pxc[z, at] = (0.5 * mask_x) * (pp[z, up] - pp[z, at])
                pxh[z, at] = (0.5 * mask_x) * (ph[z, up] - ph[z, at])
            return carry

        lax.fori_loop(0, DEPTH // STATIC_STEP, along_x, 0)

    for start in (0, 8, 16, 24, 32):
        at = pl.ds(start, 8)

        def along_yz(i, carry, at=at):
            for j in range(STATIC_STEP):
                z = i * STATIC_STEP + j
                later = jnp.minimum(z + 1, DEPTH - 1)
                inside = jnp.where(z < DEPTH - 1, 1.0, 0.0).astype(f32)
                c, h, p, q = kk[z, at], kh[z, at], pp[z, at], ph[z, at]
                cn, hn = columns_on(c, h, last)
                pn, qn = columns_on(p, q, last)
                eyc[z, at] = (half * mask_c) * (c + cn)
                eyh[z, at] = (half * mask_h) * (h + hn)
                pyc[z, at] = (0.5 * mask_c) * (pn - p)
                pyh[z, at] = (0.5 * mask_h) * (qn - q)
                ezc[z, at] = (half * inside) * (c + kk[later, at])
                ezh[z, at] = (half * inside) * (h + kh[later, at])
                pzc[z, at] = (0.5 * inside) * (pp[later, at] - p)
                pzh[z, at] = (0.5 * inside) * (ph[later, at] - q)
            return carry

        lax.fori_loop(0, DEPTH // STATIC_STEP, along_yz, 0)

    copy = pltpu.make_async_copy(built, out, sem)
    copy.start()
    copy.wait()


def statics(where, kap, prs, rows, strip):
    field = (DEPTH, EXT_ROWS, COLS)
    return pl.pallas_call(
        statics_kernel,
        out_shape=jax.ShapeDtypeStruct((FIELDS,) + field, f32),
        in_specs=[SMEM] + [VMEM] * 4,
        out_specs=HBM,
        scratch_shapes=[
            pltpu.VMEM((FIELDS,) + field, f32),
            pltpu.VMEM(field, f32),
            pltpu.VMEM(field, f32),
            pltpu.SemaphoreType.DMA,
        ],
        compiler_params=params(52),
        cost_estimate=pl.CostEstimate(
            flops=20_000_000, bytes_accessed=12_000_000, transcendentals=0
        ),
        name="statics",
    )(where, kap, prs, rows, strip)


def grid_kernel(where, basis_z, layers, kap, fields, out, built, uc, uh, vc, vh, sens, sems):
    kk, kh, pxc, pxh, pyc, pyh, pzc, pzh, exc, exh, eyc, eyh, ezc, ezh = (
        built.at[n] for n in range(FIELDS)
    )
    copies = [
        pltpu.make_async_copy(
            fields.at[pl.ds(first, size)], built.at[pl.ds(first, size)], sems.at[n]
        )
        for n, (first, size) in enumerate(((0, 2), (2, 6), (8, 6)))
    ]
    for copy in copies:
        copy.start()
    copies[0].wait()
    zh = where[1]
    lane = lax.broadcasted_iota(jnp.int32, (8, COLS), 1)
    first, last = lane == 0, lane == COLS - 1
    tiles = (EXT_ROWS + STRIP) // 8

    def layers_of(i, carry):
        for d in range(DIRECTIONS):
            totals = [[None] * tiles for _ in range(LAYER_STEP)]
            for c in range(MODES_Z):
                parts = [layers[d * MODES_Z + c, pl.ds(8 * t, 8)] for t in range(tiles)]
                for j in range(LAYER_STEP):
                    weight = basis_z[i * LAYER_STEP + j, c]
                    for t in range(tiles):
                        term = weight * parts[t]
                        totals[j][t] = term if c == 0 else totals[j][t] + term
            for j in range(LAYER_STEP):
                z = i * LAYER_STEP + j
                packed = totals[j][tiles - 1]
                for g in range(GROUPS):
                    tile = pltpu.roll(packed, strip_shift(zh, 8 * g), 1)
                    if g < ROWS // 8:
                        at = pl.ds(HALO + 8 * g, 8)
                        uc[d, z, at] = kk[z, at] * totals[j][g]
                        uh[d, z, at] = kh[z, at] * tile
                    else:
                        low, high = pl.ds(0, HALO), pl.ds(HALO + ROWS, HALO)
                        uc[d, z, low] = kk[z, low] * totals[j][g][HALO:]
                        uh[d, z, low] = kh[z, low] * tile[HALO:]
                        uc[d, z, high] = kk[z, high] * totals[j][g][:HALO]
                        uh[d, z, high] = kh[z, high] * tile[:HALO]
        return carry

    lax.fori_loop(0, DEPTH // LAYER_STEP, layers_of, 0)

    def columns_back(c, h):
        c, h = pltpu.roll(c, 1, 1), pltpu.roll(h, 1, 1)
        return jnp.where(first, h, c), jnp.where(first, c, h)

    zero = jnp.zeros((8, COLS), f32)

    def sweep(starts, source, target, coeffs, join, scale):
        (src_c, src_h), (dst_c, dst_h) = source, target
        (axc, axh), (ayc, ayh), (azc, azh) = coeffs
        for start in starts:
            at, up, down = pl.ds(start, 8), pl.ds(start + 1, 8), pl.ds(start - 1, 8)

            def body(i, carry, at=at, up=up, down=down):
                carry = list(carry)
                for j in range(PER_STEP):
                    z = i * PER_STEP + j
                    later = jnp.minimum(z + 1, DEPTH - 1)
                    for d in range(DIRECTIONS):
                        c, h, fzc, fzh = carry[4 * d : 4 * d + 4]
                        cz, hz = src_c[d, later, at], src_h[d, later, at]
                        cy, hy = columns_on(c, h, last)
                        fyc, fyh = join(cy, c) * ayc[z, at], join(hy, h) * ayh[z, at]
                        byc, byh = columns_back(fyc, fyh)
                        gzc, gzh = join(cz, c) * azc[z, at], join(hz, h) * azh[z, at]
                        xc = (
                            join(src_c[d, z, up], c) * axc[z, at]
                            - join(c, src_c[d, z, down]) * axc[z, down]
                        )
                        xh = (
                            join(src_h[d, z, up], h) * axh[z, at]
                            - join(h, src_h[d, z, down]) * axh[z, down]
                        )
                        total_c = xc + (fyc - byc) + (gzc - fzc)
                        total_h = xh + (fyh - byh) + (gzh - fzh)
                        if scale is not None:
                            total_c = scale * c + total_c
                            total_h = scale * h + total_h
                        dst_c[d, z, at] = total_c
                        dst_h[d, z, at] = total_h
                        carry[4 * d : 4 * d + 4] = [cz, hz, gzc, gzh]
                return tuple(carry)

            begin = []
            for d in range(DIRECTIONS):
                begin += [src_c[d, 0, at], src_h[d, 0, at], zero, zero]
            lax.fori_loop(0, DEPTH // PER_STEP, body, tuple(begin))

    def plus(a, b):
        return a + b

    def minus(a, b):
        return a - b

    u, v = (uc, uh), (vc, vh)
    ps = ((pxc, pxh), (pyc, pyh), (pzc, pzh))
    es = ((exc, exh), (eyc, eyh), (ezc, ezh))
    copies[1].wait()
    sweep((1, 9, 17, 25, 31), u, v, ps, plus, None)
    copies[2].wait()
    sweep((2, 10, 18, 26, 30), v, u, es, minus, 2.0 * step_size)
    sweep((3, 11, 19, 27, 29), u, v, es, minus, 2.0 * step_size)

    for start in (4, 12, 20, 28):
        at, up, down = pl.ds(start, 8), pl.ds(start + 1, 8), pl.ds(start - 1, 8)
        own = pl.ds(start - HALO, 8)

        def couple(i, carry, at=at, up=up, down=down, own=own):
            carry = list(carry)
            for j in range(PER_STEP):
                z = i * PER_STEP + j
                later = jnp.minimum(z + 1, DEPTH - 1)
                for d in range(DIRECTIONS):
                    c, fzc = carry[2 * d : 2 * d + 2]
                    h = vh[d, z, at]
                    cz = vc[d, later, at]
                    cy, hy = columns_on(c, h, last)
                    fyc, fyh = (cy - c) * pyc[z, at], (hy - h) * pyh[z, at]
                    byc, _ = columns_back(fyc, fyh)
                    gzc = (cz - c) * pzc[z, at]
                    xc = (vc[d, z, up] - c) * pxc[z, at] + (c - vc[d, z, down]) * pxc[z, down]
                    sens[d, z, own] = -kap[z, own] * (xc + (fyc + byc) + (gzc + fzc))
                    carry[2 * d : 2 * d + 2] = [cz, gzc]
            return tuple(carry)

        begin = []
        for d in range(DIRECTIONS):
            begin += [vc[d, 0, at], zero]
        lax.fori_loop(0, DEPTH // PER_STEP, couple, tuple(begin))

    def modes_of(c, carry):
        for d in range(DIRECTIONS):
            total = basis_z[0, c] * sens[d, 0]
            for z in range(1, DEPTH):
                total = total + basis_z[z, c] * sens[d, z]
            out[d * MODES_Z + c] = total
        return carry

    lax.fori_loop(0, MODES_Z, modes_of, 0)


def on_grid(where, basis_z, layers, kap, fields):
    wide = (DIRECTIONS, DEPTH, EXT_ROWS, COLS)
    return pl.pallas_call(
        grid_kernel,
        out_shape=jax.ShapeDtypeStruct((DIRECTIONS * MODES_Z, ROWS, COLS), f32),
        in_specs=[SMEM, SMEM, VMEM, VMEM, HBM],
        out_specs=VMEM,
        scratch_shapes=[pltpu.VMEM((FIELDS, DEPTH, EXT_ROWS, COLS), f32)]
        + [pltpu.VMEM(wide, f32) for _ in range(4)]
        + [
            pltpu.VMEM((DIRECTIONS, DEPTH, ROWS, COLS), f32),
            pltpu.SemaphoreType.DMA((3,)),
        ],
        compiler_params=params(52),
        cost_estimate=pl.CostEstimate(
            flops=100_000_000, bytes_accessed=12_000_000, transcendentals=0
        ),
        name="on_grid",
    )(where, basis_z, layers, kap, fields)


def project_kernel(where, values, basis, first_basis, out, blocks, sems):
    zl = where[2]
    copies = []
    for y in range(4):
        start = pl.multiple_of((y * 4 + zl) * BLOCK, BLOCK)
        copies.append(
            pltpu.make_async_copy(
                first_basis.at[pl.ds(start, BLOCK)], blocks.at[pl.ds(y * BLOCK, BLOCK)], sems.at[y]
            )
        )
    for copy in copies:
        copy.start()
    for copy in copies:
        copy.wait()
    along_x = lax.dot_general(
        blocks[...], values[...], (((0,), (0,)), ((), ())),
        precision=highest, preferred_element_type=f32,
    )
    full = lax.dot_general(
        along_x, basis[...], (((1,), (0,)), ((), ())),
        precision=highest, preferred_element_type=f32,
    )
    for y in range(4):
        for z in range(4):
            at = y * 64 + z * 16
            for h in range(2):
                out[z * 2 + h, pl.ds(y * 16, 16)] = full[at : at + 16, h * 128 : (h + 1) * 128]


def project(where, values, basis, first_basis):
    return pl.pallas_call(
        project_kernel,
        out_shape=jax.ShapeDtypeStruct((8, 64, 128), f32),
        in_specs=[SMEM, VMEM, VMEM, HBM],
        out_specs=VMEM,
        scratch_shapes=[
            pltpu.VMEM((4 * BLOCK, MODES), f32),
            pltpu.SemaphoreType.DMA((4,)),
        ],
        compiler_params=params(52),
        cost_estimate=pl.CostEstimate(
            flops=6 * 2 * 256 * 128 * 1280, bytes_accessed=2_000_000, transcendentals=0
        ),
        name="project",
    )(where, values, basis, first_basis)


def exchanged(values, axes):
    return lax.all_to_all(values, axes, split_axis=0, concat_axis=0, tiled=True)


def per_device(coefficients, first_axis_basis, basis_y, basis_z, conductivity, pressure):
    gx = lax.axis_index(GX)
    zh = lax.axis_index("zh")
    where = jnp.stack([gx, zh, lax.axis_index("zl")]).astype(jnp.int32)
    swap = [(0, 1), (1, 0)]

    flat = coefficients.reshape(DIRECTIONS * MODES_Z, 2, MODES)
    spread = jnp.broadcast_to(flat.reshape(4, 1, 8, 2, MODES), (4, 4, 8, 2, MODES))
    gathered = exchanged(spread.reshape(128, 2, MODES), GX)

    beside = lax.ppermute(
        lax.dynamic_slice_in_dim(basis_y, (COLS - STRIP) * (1 - zh), STRIP, 0), "zh", swap
    )
    both = jnp.stack([conductivity, pressure])
    upper = lax.ppermute(both[:, :, :HALO], GX, [((i + 1) % 128, i) for i in range(128)])
    lower = lax.ppermute(both[:, :, -HALO:], GX, [(i, (i + 1) % 128) for i in range(128)])
    rows, strip = pack(where, conductivity, pressure, upper, lower)
    gathered, rows = lax.optimization_barrier((gathered, rows))
    strip = lax.ppermute(strip, "zh", swap)

    message = expand(where, gathered.reshape(MODES, MODES), basis_y, beside, first_axis_basis)
    fields = statics(where, conductivity, pressure, rows, strip)
    layers = exchanged(message, PLANE)
    modes = on_grid(where, basis_z, layers, conductivity, fields)
    columns = exchanged(modes, PLANE)
    shares = project(where, columns.reshape(4 * BLOCK, COLS), basis_y, first_axis_basis)
    summed = jnp.sum(exchanged(shares, RING), axis=0)
    result = exchanged(summed.reshape(32, 2, 128), PLANE)
    own = lax.dynamic_slice_in_dim(coefficients, zh * 128, 128, 3)
    return result.reshape(DIRECTIONS, MODES_Z, 2, 128) + own


def solution(mesh):
    split = Mesh(mesh.devices.reshape(SIZES), AXES)
    return jax.shard_map(
        per_device,
        mesh=split,
        in_specs=(
            P(None, None, GX, None),
            P(),
            P("zh", None),
            P(),
            P(None, GX, "zh"),
            P(None, GX, "zh"),
        ),
        out_specs=P(None, None, GX, "zh"),
        check_vma=False,
    )
```

```python
import jax
import jax.numpy as jnp
from jax import lax
from jax.experimental import pallas as pl
from jax.experimental.pallas import tpu as pltpu
from jax.sharding import Mesh, PartitionSpec as P

step_size = 0.05
highest = lax.Precision.HIGHEST
f32 = jnp.float32

AXES = ("y", "zl", "x", "core", "zh")
SIZES = (4, 4, 4, 2, 2)
GX = ("y", "zl", "x", "core")
PLANE = ("y", "x", "core")
RING = ("zl", "zh")

DIRECTIONS, MODES_Z, DEPTH = 2, 16, 32
ROWS, COLS = 32, 128
HALO = 4
EXT_ROWS = ROWS + 2 * HALO
EXT_COLS = 2 * COLS
STRIP = 8
GROUPS = EXT_ROWS // STRIP
PER_STEP = 16
LAYER_STEP = 4
STATIC_STEP = 8
STATIC_PARTS = 4
MODES = 256
FIELDS = 14
BLOCK = 8 * ROWS
VMEM = pl.BlockSpec(memory_space=pltpu.VMEM)
SMEM = pl.BlockSpec(memory_space=pltpu.SMEM)
HBM = pl.BlockSpec(memory_space=pltpu.HBM)


def params(mib):
    return pltpu.CompilerParams(vmem_limit_bytes=mib * 1024 * 1024)


def strip_shift(zh, lane):
    return lax.rem(120 * zh + 2 * COLS - lane, COLS)


def columns_on(c, h, last):
    c, h = pltpu.roll(c, COLS - 1, 1), pltpu.roll(h, COLS - 1, 1)
    return jnp.where(last, h, c), jnp.where(last, c, h)


def pack_kernel(where, kap, prs, upper, lower, rows_out, strip_out):
    zh = where[1]
    lane = lax.broadcasted_iota(jnp.int32, (STRIP, COLS), 1)

    def body(i, carry):
        for j in range(LAYER_STEP):
            z = i * LAYER_STEP + j
            packed = jnp.zeros((STRIP, COLS), f32)
            for f, ref in enumerate((kap, prs)):
                beside = jnp.concatenate([upper[f, z], lower[f, z]], axis=0)
                rows_out[f, z] = beside
                for g in range(GROUPS):
                    tile = ref[z, pl.ds(8 * g, 8)] if g < ROWS // 8 else beside
                    first = f * EXT_ROWS + 8 * g
                    moved = pltpu.roll(tile, lax.rem(first + 8 * (1 - zh), COLS), 1)
                    packed = jnp.where((lane >= first) & (lane < first + 8), moved, packed)
            strip_out[z] = packed
        return carry

    lax.fori_loop(0, DEPTH // LAYER_STEP, body, 0)


def pack(where, kap, prs, upper, lower):
    return pl.pallas_call(
        pack_kernel,
        out_shape=(
            jax.ShapeDtypeStruct((2, DEPTH, 2 * HALO, COLS), f32),
            jax.ShapeDtypeStruct((DEPTH, STRIP, COLS), f32),
        ),
        in_specs=[SMEM] + [VMEM] * 4,
        out_specs=(VMEM, VMEM),
        compiler_params=params(61),
        cost_estimate=pl.CostEstimate(flops=2_000_000, bytes_accessed=100_000_000, transcendentals=0),
        name="pack",
    )(where, kap, prs, upper, lower)


def expand_kernel(where, coefs, basis, beside, first_basis, out, wide, blocks, sems):
    zl = where[2]
    copies = []
    for y in range(4):
        start = pl.multiple_of((y * 4 + zl) * BLOCK, BLOCK)
        below = pl.multiple_of(jnp.maximum(start - 8, 0), 8)
        above = pl.multiple_of(jnp.minimum(start + BLOCK, 4096 - 8), 8)
        for part, (src, size, dst) in enumerate(
            ((below, 8, 0), (start, BLOCK, 8), (above, 8, BLOCK + 8))
        ):
            copies.append(
                pltpu.make_async_copy(
                    first_basis.at[pl.ds(src, size)],
                    blocks.at[y, pl.ds(dst, size)],
                    sems.at[y, part],
                )
            )
    for copy in copies:
        copy.start()
    wide[pl.ds(0, COLS)] = basis[...]
    wide[pl.ds(COLS, STRIP)] = beside[...]
    wide[pl.ds(COLS + STRIP, COLS - STRIP)] = jnp.zeros((COLS - STRIP, MODES), f32)
    columns = lax.dot_general(
        coefs[...], wide[...], (((1,), (1,)), ((), ())),
        precision=highest, preferred_element_type=f32,
    )
    lane = lax.broadcasted_iota(jnp.int32, (STRIP, COLS), 1)
    low = lax.broadcasted_iota(jnp.int32, (STRIP, EXT_COLS), 0) < HALO
    for copy in copies:
        copy.wait()
    for y in range(4):
        full = lax.dot_general(
            blocks[y], columns, (((1,), (0,)), ((), ())),
            precision=highest, preferred_element_type=f32,
        )
        for k in range(8):
            own = full[8 + ROWS * k : 8 + ROWS * (k + 1)]
            above = full[8 + ROWS * (k + 1) : 16 + ROWS * (k + 1)]
            below = full[ROWS * k : ROWS * k + 8]
            ends = jnp.where(low, above, below)
            q = y * 8 + k
            out[q, pl.ds(0, ROWS)] = own[:, :COLS]
            out[q, pl.ds(ROWS, 8)] = ends[:, :COLS]
            packed = own[:8, COLS:]
            for g in range(1, GROUPS):
                tile = (own[8 * g : 8 * g + 8] if g < ROWS // 8 else ends)[:, COLS:]
                packed = jnp.where(lane < 8 * g, packed, pltpu.roll(tile, 8 * g, 1))
            out[q, pl.ds(EXT_ROWS, STRIP)] = packed


def expand(where, coefs, basis, beside, first_basis):
    return pl.pallas_call(
        expand_kernel,
        out_shape=jax.ShapeDtypeStruct((32, EXT_ROWS + STRIP, COLS), f32),
        in_specs=[SMEM, VMEM, VMEM, VMEM, HBM],
        out_specs=VMEM,
        scratch_shapes=[
            pltpu.VMEM((EXT_COLS, MODES), f32),
            pltpu.VMEM((4, BLOCK + 16, MODES), f32),
            pltpu.SemaphoreType.DMA((4, 3)),
        ],
        compiler_params=params(61),
        cost_estimate=pl.CostEstimate(
            flops=6 * 2 * 256 * 256 * 1344, bytes_accessed=40_000_000, transcendentals=0
        ),
        name="expand",
    )(where, coefs, basis, beside, first_basis)


def statics_kernel(
    where, kap, prs, rows, strip, first_basis, out, plane_rows, built, pp, ph, sems, row_sems
):
    kk, kh, pxc, pxh, pyc, pyh, pzc, pzh, exc, exh, eyc, eyh, ezc, ezh = (
        built.at[n] for n in range(FIELDS)
    )
    gx, zh, zl = where[0], where[1], where[2]
    half = 0.5 * step_size * step_size
    row_copies = [
        pltpu.make_async_copy(
            first_basis.at[pl.ds(pl.multiple_of((y * 4 + zl) * BLOCK, BLOCK), BLOCK)],
            plane_rows.at[pl.ds(y * BLOCK, BLOCK)],
            row_sems.at[y],
        )
        for y in range(4)
    ]
    for copy in row_copies:
        copy.start()

    def place(i, carry):
        for j in range(STATIC_STEP):
            z = i * STATIC_STEP + j
            packed = strip[z]
            for f, (src, dst, far) in enumerate(((kap, kk, kh), (prs, pp, ph))):
                ends = rows[f, z]
                dst[z, pl.ds(HALO, ROWS)] = src[z]
                dst[z, pl.ds(0, HALO)] = ends[HALO:]
                dst[z, pl.ds(HALO + ROWS, HALO)] = ends[:HALO]
                for g in range(GROUPS):
                    tile = pltpu.roll(packed, strip_shift(zh, f * EXT_ROWS + 8 * g), 1)
                    if g < ROWS // 8:
                        far[z, pl.ds(HALO + 8 * g, 8)] = tile
                    else:
                        far[z, pl.ds(0, HALO)] = tile[HALO:]
                        far[z, pl.ds(HALO + ROWS, HALO)] = tile[:HALO]
        return carry

    lax.fori_loop(0, DEPTH // STATIC_STEP, place, 0)

    lane = lax.broadcasted_iota(jnp.int32, (8, COLS), 1)
    row = lax.broadcasted_iota(jnp.int32, (8, COLS), 0)
    last = lane == COLS - 1
    mask_c = jnp.where(last & (zh == 1), 0.0, 1.0).astype(f32)
    mask_h = jnp.where(last & (zh == 0), 0.0, 1.0).astype(f32)
    lowest, highest_row = jnp.where(gx == 0, HALO - 1, -1), jnp.where(gx == 127, HALO + ROWS - 1, -1)

    copies = []
    span = DEPTH // STATIC_PARTS
    for part in range(STATIC_PARTS):
        begin, end = part * span // STATIC_STEP, (part + 1) * span // STATIC_STEP
        for start in (0, 8, 16, 24, 31):
            at, up = pl.ds(start, 8), pl.ds(start + 1, 8)
            here = row + start
            mask_x = jnp.where((here == lowest) | (here == highest_row), 0.0, 1.0).astype(f32)

            def along_x(i, carry, at=at, up=up, mask_x=mask_x):
                for j in range(STATIC_STEP):
                    z = i * STATIC_STEP + j
                    exc[z, at] = (half * mask_x) * (kk[z, at] + kk[z, up])
                    exh[z, at] = (half * mask_x) * (kh[z, at] + kh[z, up])
                    pxc[z, at] = (0.5 * mask_x) * (pp[z, up] - pp[z, at])
                    pxh[z, at] = (0.5 * mask_x) * (ph[z, up] - ph[z, at])
                return carry

            lax.fori_loop(begin, end, along_x, 0)

        for start in (0, 8, 16, 24, 32):
            at = pl.ds(start, 8)

            def along_yz(i, carry, at=at):
                for j in range(STATIC_STEP):
                    z = i * STATIC_STEP + j
                    later = jnp.minimum(z + 1, DEPTH - 1)
                    inside = jnp.where(z < DEPTH - 1, 1.0, 0.0).astype(f32)
                    c, h, p, q = kk[z, at], kh[z, at], pp[z, at], ph[z, at]
                    cn, hn = columns_on(c, h, last)
                    pn, qn = columns_on(p, q, last)
                    eyc[z, at] = (half * mask_c) * (c + cn)
                    eyh[z, at] = (half * mask_h) * (h + hn)
                    pyc[z, at] = (0.5 * mask_c) * (pn - p)
                    pyh[z, at] = (0.5 * mask_h) * (qn - q)
                    ezc[z, at] = (half * inside) * (c + kk[later, at])
                    ezh[z, at] = (half * inside) * (h + kh[later, at])
                    pzc[z, at] = (0.5 * inside) * (pp[later, at] - p)
                    pzh[z, at] = (0.5 * inside) * (ph[later, at] - q)
                return carry

            lax.fori_loop(begin, end, along_yz, 0)

        copies.append(
            pltpu.make_async_copy(
                built.at[:, pl.ds(part * span, span)], out.at[:, pl.ds(part * span, span)], sems.at[part]
            )
        )
        copies[-1].start()
    for copy in copies + row_copies:
        copy.wait()


def statics(where, kap, prs, rows, strip, first_basis):
    field = (DEPTH, EXT_ROWS, COLS)
    return pl.pallas_call(
        statics_kernel,
        out_shape=(
            jax.ShapeDtypeStruct((FIELDS,) + field, f32),
            jax.ShapeDtypeStruct((4 * BLOCK, MODES), f32),
        ),
        in_specs=[SMEM] + [VMEM] * 4 + [HBM],
        out_specs=(HBM, HBM),
        scratch_shapes=[
            pltpu.VMEM((FIELDS,) + field, f32),
            pltpu.VMEM(field, f32),
            pltpu.VMEM(field, f32),
            pltpu.SemaphoreType.DMA((STATIC_PARTS,)),
            pltpu.SemaphoreType.DMA((4,)),
        ],
        compiler_params=params(52),
        cost_estimate=pl.CostEstimate(
            flops=20_000_000, bytes_accessed=150_000_000, transcendentals=0
        ),
        name="statics",
    )(where, kap, prs, rows, strip, first_basis)


def grid_kernel(where, basis_z, layers, kap, fields, out, built, uc, uh, vc, vh, sens, sems):
    kk, kh, pxc, pxh, pyc, pyh, pzc, pzh, exc, exh, eyc, eyh, ezc, ezh = (
        built.at[n] for n in range(FIELDS)
    )
    copies = [
        pltpu.make_async_copy(
            fields.at[pl.ds(first, size)], built.at[pl.ds(first, size)], sems.at[n]
        )
        for n, (first, size) in enumerate(((0, 2), (2, 6), (8, 6)))
    ]
    for copy in copies:
        copy.start()
    copies[0].wait()
    zh = where[1]
    lane = lax.broadcasted_iota(jnp.int32, (8, COLS), 1)
    first, last = lane == 0, lane == COLS - 1
    tiles = (EXT_ROWS + STRIP) // 8

    def layers_of(i, carry):
        for d in range(DIRECTIONS):
            totals = [[None] * tiles for _ in range(LAYER_STEP)]
            for c in range(MODES_Z):
                parts = [layers[d * MODES_Z + c, pl.ds(8 * t, 8)] for t in range(tiles)]
                for j in range(LAYER_STEP):
                    weight = basis_z[i * LAYER_STEP + j, c]
                    for t in range(tiles):
                        term = weight * parts[t]
                        totals[j][t] = term if c == 0 else totals[j][t] + term
            for j in range(LAYER_STEP):
                z = i * LAYER_STEP + j
                packed = totals[j][tiles - 1]
                for g in range(GROUPS):
                    tile = pltpu.roll(packed, strip_shift(zh, 8 * g), 1)
                    if g < ROWS // 8:
                        at = pl.ds(HALO + 8 * g, 8)
                        uc[d, z, at] = kk[z, at] * totals[j][g]
                        uh[d, z, at] = kh[z, at] * tile
                    else:
                        low, high = pl.ds(0, HALO), pl.ds(HALO + ROWS, HALO)
                        uc[d, z, low] = kk[z, low] * totals[j][g][HALO:]
                        uh[d, z, low] = kh[z, low] * tile[HALO:]
                        uc[d, z, high] = kk[z, high] * totals[j][g][:HALO]
                        uh[d, z, high] = kh[z, high] * tile[:HALO]
        return carry

    lax.fori_loop(0, DEPTH // LAYER_STEP, layers_of, 0)

    def columns_back(c, h):
        c, h = pltpu.roll(c, 1, 1), pltpu.roll(h, 1, 1)
        return jnp.where(first, h, c), jnp.where(first, c, h)

    zero = jnp.zeros((8, COLS), f32)

    def sweep(starts, source, target, coeffs, join, scale):
        (src_c, src_h), (dst_c, dst_h) = source, target
        (axc, axh), (ayc, ayh), (azc, azh) = coeffs
        for start in starts:
            at, up, down = pl.ds(start, 8), pl.ds(start + 1, 8), pl.ds(start - 1, 8)

            def body(i, carry, at=at, up=up, down=down):
                carry = list(carry)
                for j in range(PER_STEP):
                    z = i * PER_STEP + j
                    later = jnp.minimum(z + 1, DEPTH - 1)
                    for d in range(DIRECTIONS):
                        c, h, fzc, fzh = carry[4 * d : 4 * d + 4]
                        cz, hz = src_c[d, later, at], src_h[d, later, at]
                        cy, hy = columns_on(c, h, last)
                        fyc, fyh = join(cy, c) * ayc[z, at], join(hy, h) * ayh[z, at]
                        byc, byh = columns_back(fyc, fyh)
                        gzc, gzh = join(cz, c) * azc[z, at], join(hz, h) * azh[z, at]
                        xc = (
                            join(src_c[d, z, up], c) * axc[z, at]
                            - join(c, src_c[d, z, down]) * axc[z, down]
                        )
                        xh = (
                            join(src_h[d, z, up], h) * axh[z, at]
                            - join(h, src_h[d, z, down]) * axh[z, down]
                        )
                        total_c = xc + (fyc - byc) + (gzc - fzc)
                        total_h = xh + (fyh - byh) + (gzh - fzh)
                        if scale is not None:
                            total_c = scale * c + total_c
                            total_h = scale * h + total_h
                        dst_c[d, z, at] = total_c
                        dst_h[d, z, at] = total_h
                        carry[4 * d : 4 * d + 4] = [cz, hz, gzc, gzh]
                return tuple(carry)

            begin = []
            for d in range(DIRECTIONS):
                begin += [src_c[d, 0, at], src_h[d, 0, at], zero, zero]
            lax.fori_loop(0, DEPTH // PER_STEP, body, tuple(begin))

    def plus(a, b):
        return a + b

    def minus(a, b):
        return a - b

    u, v = (uc, uh), (vc, vh)
    ps = ((pxc, pxh), (pyc, pyh), (pzc, pzh))
    es = ((exc, exh), (eyc, eyh), (ezc, ezh))
    copies[1].wait()
    sweep((1, 9, 17, 25, 31), u, v, ps, plus, None)
    copies[2].wait()
    sweep((2, 10, 18, 26, 30), v, u, es, minus, 2.0 * step_size)
    sweep((3, 11, 19, 27, 29), u, v, es, minus, 2.0 * step_size)

    for start in (4, 12, 20, 28):
        at, up, down = pl.ds(start, 8), pl.ds(start + 1, 8), pl.ds(start - 1, 8)
        own = pl.ds(start - HALO, 8)

        def couple(i, carry, at=at, up=up, down=down, own=own):
            carry = list(carry)
            for j in range(PER_STEP):
                z = i * PER_STEP + j
                later = jnp.minimum(z + 1, DEPTH - 1)
                for d in range(DIRECTIONS):
                    c, fzc = carry[2 * d : 2 * d + 2]
                    h = vh[d, z, at]
                    cz = vc[d, later, at]
                    cy, hy = columns_on(c, h, last)
                    fyc, fyh = (cy - c) * pyc[z, at], (hy - h) * pyh[z, at]
                    byc, _ = columns_back(fyc, fyh)
                    gzc = (cz - c) * pzc[z, at]
                    xc = (vc[d, z, up] - c) * pxc[z, at] + (c - vc[d, z, down]) * pxc[z, down]
                    sens[d, z, own] = -kap[z, own] * (xc + (fyc + byc) + (gzc + fzc))
                    carry[2 * d : 2 * d + 2] = [cz, gzc]
            return tuple(carry)

        begin = []
        for d in range(DIRECTIONS):
            begin += [vc[d, 0, at], zero]
        lax.fori_loop(0, DEPTH // PER_STEP, couple, tuple(begin))

    def modes_of(c, carry):
        for d in range(DIRECTIONS):
            total = basis_z[0, c] * sens[d, 0]
            for z in range(1, DEPTH):
                total = total + basis_z[z, c] * sens[d, z]
            out[d * MODES_Z + c] = total
        return carry

    lax.fori_loop(0, MODES_Z, modes_of, 0)


def on_grid(where, basis_z, layers, kap, fields):
    wide = (DIRECTIONS, DEPTH, EXT_ROWS, COLS)
    return pl.pallas_call(
        grid_kernel,
        out_shape=jax.ShapeDtypeStruct((DIRECTIONS * MODES_Z, ROWS, COLS), f32),
        in_specs=[SMEM, SMEM, VMEM, VMEM, HBM],
        out_specs=VMEM,
        scratch_shapes=[pltpu.VMEM((FIELDS, DEPTH, EXT_ROWS, COLS), f32)]
        + [pltpu.VMEM(wide, f32) for _ in range(4)]
        + [
            pltpu.VMEM((DIRECTIONS, DEPTH, ROWS, COLS), f32),
            pltpu.SemaphoreType.DMA((3,)),
        ],
        compiler_params=params(52),
        cost_estimate=pl.CostEstimate(
            flops=100_000_000, bytes_accessed=12_000_000, transcendentals=0
        ),
        name="on_grid",
    )(where, basis_z, layers, kap, fields)


def project_kernel(values, basis, plane_rows, out):
    along_x = lax.dot_general(
        plane_rows[...], values[...], (((0,), (0,)), ((), ())),
        precision=highest, preferred_element_type=f32,
    )
    full = lax.dot_general(
        along_x, basis[...], (((1,), (0,)), ((), ())),
        precision=highest, preferred_element_type=f32,
    )
    for y in range(4):
        for z in range(4):
            at = y * 64 + z * 16
            for h in range(2):
                out[z * 2 + h, pl.ds(y * 16, 16)] = full[at : at + 16, h * 128 : (h + 1) * 128]


def project(values, basis, plane_rows):
    return pl.pallas_call(
        project_kernel,
        out_shape=jax.ShapeDtypeStruct((8, 64, 128), f32),
        in_specs=[VMEM, VMEM, VMEM],
        out_specs=VMEM,
        compiler_params=params(48),
        cost_estimate=pl.CostEstimate(
            flops=6 * 2 * 256 * 128 * 1280, bytes_accessed=2_000_000, transcendentals=0
        ),
        name="project",
    )(values, basis, plane_rows)


def exchanged(values, axes):
    return lax.all_to_all(values, axes, split_axis=0, concat_axis=0, tiled=True)


def per_device(coefficients, first_axis_basis, basis_y, basis_z, conductivity, pressure):
    gx = lax.axis_index(GX)
    zh = lax.axis_index("zh")
    where = jnp.stack([gx, zh, lax.axis_index("zl")]).astype(jnp.int32)
    swap = [(0, 1), (1, 0)]

    flat = coefficients.reshape(DIRECTIONS * MODES_Z, 2, MODES)
    spread = jnp.broadcast_to(flat.reshape(4, 1, 8, 2, MODES), (4, 4, 8, 2, MODES))
    gathered = exchanged(spread.reshape(128, 2, MODES), GX)

    edges = jnp.concatenate([basis_y[:STRIP] * zh, basis_y[-STRIP:] * (1 - zh)])
    beside = lax.psum_scatter(edges, "zh", scatter_dimension=0, tiled=True)
    both = jnp.stack([conductivity, pressure])
    upper = lax.ppermute(both[:, :, :HALO], GX, [((i + 1) % 128, i) for i in range(128)])
    lower = lax.ppermute(both[:, :, -HALO:], GX, [(i, (i + 1) % 128) for i in range(128)])
    rows, strip = pack(where, conductivity, pressure, upper, lower)
    gathered, rows = lax.optimization_barrier((gathered, rows))
    strip = lax.ppermute(strip, "zh", swap)

    message = expand(where, gathered.reshape(MODES, MODES), basis_y, beside, first_axis_basis)
    message, strip = lax.optimization_barrier((message, strip))
    fields, plane_rows = statics(where, conductivity, pressure, rows, strip, first_axis_basis)
    layers = exchanged(message, PLANE)
    modes = on_grid(where, basis_z, layers, conductivity, fields)
    columns = exchanged(modes, PLANE)
    shares = project(columns.reshape(4 * BLOCK, COLS), basis_y, plane_rows)
    summed = jnp.sum(exchanged(shares, RING), axis=0)
    result = exchanged(summed.reshape(32, 2, 128), PLANE)
    own = lax.dynamic_slice_in_dim(coefficients, zh * 128, 128, 3)
    return result.reshape(DIRECTIONS, MODES_Z, 2, 128) + own


def solution(mesh):
    split = Mesh(mesh.devices.reshape(SIZES), AXES)
    return jax.shard_map(
        per_device,
        mesh=split,
        in_specs=(
            P(None, None, GX, None),
            P(),
            P("zh", None),
            P(),
            P(None, GX, "zh"),
            P(None, GX, "zh"),
        ),
        out_specs=P(None, None, GX, "zh"),
        check_vma=False,
    )
```

```python
import jax
import jax.numpy as jnp
from jax import lax
from jax.experimental import pallas as pl
from jax.experimental.pallas import tpu as pltpu
from jax.sharding import Mesh, PartitionSpec as P

step_size = 0.05
highest = lax.Precision.HIGHEST
f32 = jnp.float32

AXES = ("y", "zl", "x", "core", "zh")
SIZES = (4, 4, 4, 2, 2)
GX = ("y", "zl", "x", "core")
PLANE = ("y", "x", "core")
RING = ("zl", "zh")

DIRECTIONS, MODES_Z, DEPTH = 2, 16, 32
ROWS, COLS = 32, 128
HALO = 4
EXT_ROWS = ROWS + 2 * HALO
EXT_COLS = 2 * COLS
STRIP = 8
GROUPS = EXT_ROWS // STRIP
PER_STEP = 16
LAYER_STEP = 4
STATIC_STEP = 8
STATIC_PARTS = 4
MODES = 256
FIELDS = 14
BLOCK = 8 * ROWS
VMEM = pl.BlockSpec(memory_space=pltpu.VMEM)
SMEM = pl.BlockSpec(memory_space=pltpu.SMEM)
HBM = pl.BlockSpec(memory_space=pltpu.HBM)


def params(mib):
    return pltpu.CompilerParams(vmem_limit_bytes=mib * 1024 * 1024)


def strip_shift(zh, lane):
    return lax.rem(120 * zh + 2 * COLS - lane, COLS)


def columns_on(c, h, last):
    c, h = pltpu.roll(c, COLS - 1, 1), pltpu.roll(h, COLS - 1, 1)
    return jnp.where(last, h, c), jnp.where(last, c, h)


def pack_kernel(where, kap, prs, basis, out):
    zh = where[1]
    lane = lax.broadcasted_iota(jnp.int32, (STRIP, COLS), 1)

    def body(i, carry):
        for j in range(LAYER_STEP):
            z = i * LAYER_STEP + j
            packed = jnp.zeros((STRIP, COLS), f32)
            for f, ref in enumerate((kap, prs)):
                for g in range(ROWS // 8):
                    first = f * ROWS + 8 * g
                    moved = pltpu.roll(
                        ref[z, pl.ds(8 * g, 8)], lax.rem(first + 8 * (1 - zh), COLS), 1
                    )
                    packed = jnp.where((lane >= first) & (lane < first + 8), moved, packed)
            out[z] = packed
        return carry

    lax.fori_loop(0, DEPTH // LAYER_STEP, body, 0)
    edge = jnp.where(zh == 0, basis[COLS - STRIP :], basis[:STRIP])
    for part in range(2):
        out[DEPTH + part] = edge[:, COLS * part : COLS * (part + 1)]


def pack(where, kap, prs, basis):
    return pl.pallas_call(
        pack_kernel,
        out_shape=jax.ShapeDtypeStruct((DEPTH + 2, STRIP, COLS), f32),
        in_specs=[SMEM] + [VMEM] * 3,
        out_specs=VMEM,
        compiler_params=params(61),
        cost_estimate=pl.CostEstimate(
            flops=2_000_000, bytes_accessed=1_300_000, transcendentals=0
        ),
        name="pack",
    )(where, kap, prs, basis)


def expand_kernel(where, coefs, basis, beside, first_basis, out, wide, blocks, sems):
    zl = where[2]
    copies = []
    for y in range(4):
        start = pl.multiple_of((y * 4 + zl) * BLOCK, BLOCK)
        below = pl.multiple_of(jnp.maximum(start - 8, 0), 8)
        above = pl.multiple_of(jnp.minimum(start + BLOCK, 4096 - 8), 8)
        for part, (src, size, dst) in enumerate(
            ((below, 8, 0), (start, BLOCK, 8), (above, 8, BLOCK + 8))
        ):
            copies.append(
                pltpu.make_async_copy(
                    first_basis.at[pl.ds(src, size)],
                    blocks.at[y, pl.ds(dst, size)],
                    sems.at[y, part],
                )
            )
    for copy in copies:
        copy.start()
    wide[pl.ds(0, COLS)] = basis[...]
    for part in range(2):
        wide[pl.ds(COLS, STRIP), pl.ds(COLS * part, COLS)] = beside[DEPTH + part]
    wide[pl.ds(COLS + STRIP, COLS - STRIP)] = jnp.zeros((COLS - STRIP, MODES), f32)
    columns = lax.dot_general(
        coefs[...], wide[...], (((1,), (1,)), ((), ())),
        precision=highest, preferred_element_type=f32,
    )
    lane = lax.broadcasted_iota(jnp.int32, (STRIP, COLS), 1)
    low = lax.broadcasted_iota(jnp.int32, (STRIP, EXT_COLS), 0) < HALO
    for copy in copies:
        copy.wait()
    for y in range(4):
        full = lax.dot_general(
            blocks[y], columns, (((1,), (0,)), ((), ())),
            precision=highest, preferred_element_type=f32,
        )
        for k in range(8):
            own = full[8 + ROWS * k : 8 + ROWS * (k + 1)]
            above = full[8 + ROWS * (k + 1) : 16 + ROWS * (k + 1)]
            below = full[ROWS * k : ROWS * k + 8]
            ends = jnp.where(low, above, below)
            q = y * 8 + k
            out[q, pl.ds(0, ROWS)] = own[:, :COLS]
            out[q, pl.ds(ROWS, 8)] = ends[:, :COLS]
            packed = own[:8, COLS:]
            for g in range(1, GROUPS):
                tile = (own[8 * g : 8 * g + 8] if g < ROWS // 8 else ends)[:, COLS:]
                packed = jnp.where(lane < 8 * g, packed, pltpu.roll(tile, 8 * g, 1))
            out[q, pl.ds(EXT_ROWS, STRIP)] = packed


def expand(where, coefs, basis, beside, first_basis):
    return pl.pallas_call(
        expand_kernel,
        out_shape=jax.ShapeDtypeStruct((32, EXT_ROWS + STRIP, COLS), f32),
        in_specs=[SMEM, VMEM, VMEM, VMEM, HBM],
        out_specs=VMEM,
        scratch_shapes=[
            pltpu.VMEM((EXT_COLS, MODES), f32),
            pltpu.VMEM((4, BLOCK + 16, MODES), f32),
            pltpu.SemaphoreType.DMA((4, 3)),
        ],
        compiler_params=params(61),
        cost_estimate=pl.CostEstimate(
            flops=6 * 2 * 256 * 256 * 1344, bytes_accessed=40_000_000, transcendentals=0
        ),
        name="expand",
    )(where, coefs, basis, beside, first_basis)


def statics_kernel(
    where, kap, prs, upper, lower, strip, first_basis, out, plane_rows,
    built, pp, ph, held, sems, row_sems,
):
    kk, kh, pxc, pxh, pyc, pyh, pzc, pzh, exc, exh, eyc, eyh, ezc, ezh = (
        built.at[n] for n in range(FIELDS)
    )
    gx, zh, zl = where[0], where[1], where[2]
    half = 0.5 * step_size * step_size
    row_copies = [
        pltpu.make_async_copy(
            first_basis.at[pl.ds(pl.multiple_of((y * 4 + zl) * BLOCK, BLOCK), BLOCK)],
            held.at[pl.ds(y * BLOCK, BLOCK)],
            row_sems.at[y],
        )
        for y in range(4)
    ]
    for copy in row_copies:
        copy.start()

    def place(i, carry):
        for j in range(STATIC_STEP):
            z = i * STATIC_STEP + j
            packed = strip[z]
            for f, (src, dst, far) in enumerate(((kap, kk, kh), (prs, pp, ph))):
                low, high = pl.ds(0, HALO), pl.ds(HALO + ROWS, HALO)
                dst[z, pl.ds(HALO, ROWS)] = src[z]
                dst[z, low] = lower[f, z]
                dst[z, high] = upper[f, z]
                for g in range(ROWS // 8):
                    far[z, pl.ds(HALO + 8 * g, 8)] = pltpu.roll(
                        packed, strip_shift(zh, f * ROWS + 8 * g), 1
                    )
                corners = jnp.concatenate([lower[2, z], upper[2, z]], axis=0)
                far[z, low] = pltpu.roll(corners, strip_shift(zh, (f + 1) * ROWS - 8), 1)[:HALO]
                far[z, high] = pltpu.roll(corners, strip_shift(zh, f * ROWS), 1)[HALO:]
        return carry

    lax.fori_loop(0, DEPTH // STATIC_STEP, place, 0)

    lane = lax.broadcasted_iota(jnp.int32, (8, COLS), 1)
    row = lax.broadcasted_iota(jnp.int32, (8, COLS), 0)
    last = lane == COLS - 1
    mask_c = jnp.where(last & (zh == 1), 0.0, 1.0).astype(f32)
    mask_h = jnp.where(last & (zh == 0), 0.0, 1.0).astype(f32)
    lowest, highest_row = jnp.where(gx == 0, HALO - 1, -1), jnp.where(gx == 127, HALO + ROWS - 1, -1)

    copies = []
    span = DEPTH // STATIC_PARTS
    for part in range(STATIC_PARTS):
        begin, end = part * span // STATIC_STEP, (part + 1) * span // STATIC_STEP
        for start in (0, 8, 16, 24, 31):
            at, up = pl.ds(start, 8), pl.ds(start + 1, 8)
            here = row + start
            mask_x = jnp.where((here == lowest) | (here == highest_row), 0.0, 1.0).astype(f32)

            def along_x(i, carry, at=at, up=up, mask_x=mask_x):
                for j in range(STATIC_STEP):
                    z = i * STATIC_STEP + j
                    exc[z, at] = (half * mask_x) * (kk[z, at] + kk[z, up])
                    exh[z, at] = (half * mask_x) * (kh[z, at] + kh[z, up])
                    pxc[z, at] = (0.5 * mask_x) * (pp[z, up] - pp[z, at])
                    pxh[z, at] = (0.5 * mask_x) * (ph[z, up] - ph[z, at])
                return carry

            lax.fori_loop(begin, end, along_x, 0)

        for start in (0, 8, 16, 24, 32):
            at = pl.ds(start, 8)

            def along_yz(i, carry, at=at):
                for j in range(STATIC_STEP):
                    z = i * STATIC_STEP + j
                    later = jnp.minimum(z + 1, DEPTH - 1)
                    inside = jnp.where(z < DEPTH - 1, 1.0, 0.0).astype(f32)
                    c, h, p, q = kk[z, at], kh[z, at], pp[z, at], ph[z, at]
                    cn, hn = columns_on(c, h, last)
                    pn, qn = columns_on(p, q, last)
                    eyc[z, at] = (half * mask_c) * (c + cn)
                    eyh[z, at] = (half * mask_h) * (h + hn)
                    pyc[z, at] = (0.5 * mask_c) * (pn - p)
                    pyh[z, at] = (0.5 * mask_h) * (qn - q)
                    ezc[z, at] = (half * inside) * (c + kk[later, at])
                    ezh[z, at] = (half * inside) * (h + kh[later, at])
                    pzc[z, at] = (0.5 * inside) * (pp[later, at] - p)
                    pzh[z, at] = (0.5 * inside) * (ph[later, at] - q)
                return carry

            lax.fori_loop(begin, end, along_yz, 0)

        copies.append(
            pltpu.make_async_copy(
                built.at[:, pl.ds(part * span, span)], out.at[:, pl.ds(part * span, span)], sems.at[part]
            )
        )
        copies[-1].start()
    for copy in row_copies:
        copy.wait()
    copies.append(pltpu.make_async_copy(held, plane_rows, row_sems.at[4]))
    copies[-1].start()
    for copy in copies:
        copy.wait()


def statics(where, kap, prs, upper, lower, strip, first_basis):
    field = (DEPTH, EXT_ROWS, COLS)
    return pl.pallas_call(
        statics_kernel,
        out_shape=(
            jax.ShapeDtypeStruct((FIELDS,) + field, f32),
            jax.ShapeDtypeStruct((4 * BLOCK, MODES), f32),
        ),
        in_specs=[SMEM] + [VMEM] * 5 + [HBM],
        out_specs=(HBM, HBM),
        scratch_shapes=[
            pltpu.VMEM((FIELDS,) + field, f32),
            pltpu.VMEM(field, f32),
            pltpu.VMEM(field, f32),
            pltpu.VMEM((4 * BLOCK, MODES), f32),
            pltpu.SemaphoreType.DMA((STATIC_PARTS,)),
            pltpu.SemaphoreType.DMA((5,)),
        ],
        compiler_params=params(52),
        cost_estimate=pl.CostEstimate(
            flops=20_000_000, bytes_accessed=150_000_000, transcendentals=0
        ),
        name="statics",
    )(where, kap, prs, upper, lower, strip, first_basis)


def grid_kernel(where, basis_z, layers, kap, fields, out, built, uc, uh, vc, vh, sens, sems):
    kk, kh, pxc, pxh, pyc, pyh, pzc, pzh, exc, exh, eyc, eyh, ezc, ezh = (
        built.at[n] for n in range(FIELDS)
    )
    copies = [
        pltpu.make_async_copy(
            fields.at[pl.ds(first, size)], built.at[pl.ds(first, size)], sems.at[n]
        )
        for n, (first, size) in enumerate(((0, 2), (2, 6), (8, 6)))
    ]
    for copy in copies:
        copy.start()
    copies[0].wait()
    zh = where[1]
    lane = lax.broadcasted_iota(jnp.int32, (8, COLS), 1)
    first, last = lane == 0, lane == COLS - 1
    tiles = (EXT_ROWS + STRIP) // 8

    def layers_of(i, carry):
        for d in range(DIRECTIONS):
            totals = [[None] * tiles for _ in range(LAYER_STEP)]
            for c in range(MODES_Z):
                parts = [layers[d * MODES_Z + c, pl.ds(8 * t, 8)] for t in range(tiles)]
                for j in range(LAYER_STEP):
                    weight = basis_z[i * LAYER_STEP + j, c]
                    for t in range(tiles):
                        term = weight * parts[t]
                        totals[j][t] = term if c == 0 else totals[j][t] + term
            for j in range(LAYER_STEP):
                z = i * LAYER_STEP + j
                packed = totals[j][tiles - 1]
                for g in range(GROUPS):
                    tile = pltpu.roll(packed, strip_shift(zh, 8 * g), 1)
                    if g < ROWS // 8:
                        at = pl.ds(HALO + 8 * g, 8)
                        uc[d, z, at] = kk[z, at] * totals[j][g]
                        uh[d, z, at] = kh[z, at] * tile
                    else:
                        low, high = pl.ds(0, HALO), pl.ds(HALO + ROWS, HALO)
                        uc[d, z, low] = kk[z, low] * totals[j][g][HALO:]
                        uh[d, z, low] = kh[z, low] * tile[HALO:]
                        uc[d, z, high] = kk[z, high] * totals[j][g][:HALO]
                        uh[d, z, high] = kh[z, high] * tile[:HALO]
        return carry

    lax.fori_loop(0, DEPTH // LAYER_STEP, layers_of, 0)

    def columns_back(c, h):
        c, h = pltpu.roll(c, 1, 1), pltpu.roll(h, 1, 1)
        return jnp.where(first, h, c), jnp.where(first, c, h)

    zero = jnp.zeros((8, COLS), f32)

    def sweep(starts, source, target, coeffs, join, scale):
        (src_c, src_h), (dst_c, dst_h) = source, target
        (axc, axh), (ayc, ayh), (azc, azh) = coeffs
        for start in starts:
            at, up, down = pl.ds(start, 8), pl.ds(start + 1, 8), pl.ds(start - 1, 8)

            def body(i, carry, at=at, up=up, down=down):
                carry = list(carry)
                for j in range(PER_STEP):
                    z = i * PER_STEP + j
                    later = jnp.minimum(z + 1, DEPTH - 1)
                    for d in range(DIRECTIONS):
                        c, h, fzc, fzh = carry[4 * d : 4 * d + 4]
                        cz, hz = src_c[d, later, at], src_h[d, later, at]
                        cy, hy = columns_on(c, h, last)
                        fyc, fyh = join(cy, c) * ayc[z, at], join(hy, h) * ayh[z, at]
                        byc, byh = columns_back(fyc, fyh)
                        gzc, gzh = join(cz, c) * azc[z, at], join(hz, h) * azh[z, at]
                        xc = (
                            join(src_c[d, z, up], c) * axc[z, at]
                            - join(c, src_c[d, z, down]) * axc[z, down]
                        )
                        xh = (
                            join(src_h[d, z, up], h) * axh[z, at]
                            - join(h, src_h[d, z, down]) * axh[z, down]
                        )
                        total_c = xc + (fyc - byc) + (gzc - fzc)
                        total_h = xh + (fyh - byh) + (gzh - fzh)
                        if scale is not None:
                            total_c = scale * c + total_c
                            total_h = scale * h + total_h
                        dst_c[d, z, at] = total_c
                        dst_h[d, z, at] = total_h
                        carry[4 * d : 4 * d + 4] = [cz, hz, gzc, gzh]
                return tuple(carry)

            begin = []
            for d in range(DIRECTIONS):
                begin += [src_c[d, 0, at], src_h[d, 0, at], zero, zero]
            lax.fori_loop(0, DEPTH // PER_STEP, body, tuple(begin))

    def plus(a, b):
        return a + b

    def minus(a, b):
        return a - b

    u, v = (uc, uh), (vc, vh)
    ps = ((pxc, pxh), (pyc, pyh), (pzc, pzh))
    es = ((exc, exh), (eyc, eyh), (ezc, ezh))
    copies[1].wait()
    sweep((1, 9, 17, 25, 31), u, v, ps, plus, None)
    copies[2].wait()
    sweep((2, 10, 18, 26, 30), v, u, es, minus, 2.0 * step_size)
    sweep((3, 11, 19, 27, 29), u, v, es, minus, 2.0 * step_size)

    for start in (4, 12, 20, 28):
        at, up, down = pl.ds(start, 8), pl.ds(start + 1, 8), pl.ds(start - 1, 8)
        own = pl.ds(start - HALO, 8)

        def couple(i, carry, at=at, up=up, down=down, own=own):
            carry = list(carry)
            for j in range(PER_STEP):
                z = i * PER_STEP + j
                later = jnp.minimum(z + 1, DEPTH - 1)
                for d in range(DIRECTIONS):
                    c, fzc = carry[2 * d : 2 * d + 2]
                    h = vh[d, z, at]
                    cz = vc[d, later, at]
                    cy, hy = columns_on(c, h, last)
                    fyc, fyh = (cy - c) * pyc[z, at], (hy - h) * pyh[z, at]
                    byc, _ = columns_back(fyc, fyh)
                    gzc = (cz - c) * pzc[z, at]
                    xc = (vc[d, z, up] - c) * pxc[z, at] + (c - vc[d, z, down]) * pxc[z, down]
                    sens[d, z, own] = -kap[z, own] * (xc + (fyc + byc) + (gzc + fzc))
                    carry[2 * d : 2 * d + 2] = [cz, gzc]
            return tuple(carry)

        begin = []
        for d in range(DIRECTIONS):
            begin += [vc[d, 0, at], zero]
        lax.fori_loop(0, DEPTH // PER_STEP, couple, tuple(begin))

    def modes_of(c, carry):
        for d in range(DIRECTIONS):
            total = basis_z[0, c] * sens[d, 0]
            for z in range(1, DEPTH):
                total = total + basis_z[z, c] * sens[d, z]
            out[d * MODES_Z + c] = total
        return carry

    lax.fori_loop(0, MODES_Z, modes_of, 0)


def on_grid(where, basis_z, layers, kap, fields):
    wide = (DIRECTIONS, DEPTH, EXT_ROWS, COLS)
    return pl.pallas_call(
        grid_kernel,
        out_shape=jax.ShapeDtypeStruct((DIRECTIONS * MODES_Z, ROWS, COLS), f32),
        in_specs=[SMEM, SMEM, VMEM, VMEM, HBM],
        out_specs=VMEM,
        scratch_shapes=[pltpu.VMEM((FIELDS, DEPTH, EXT_ROWS, COLS), f32)]
        + [pltpu.VMEM(wide, f32) for _ in range(4)]
        + [
            pltpu.VMEM((DIRECTIONS, DEPTH, ROWS, COLS), f32),
            pltpu.SemaphoreType.DMA((3,)),
        ],
        compiler_params=params(52),
        cost_estimate=pl.CostEstimate(
            flops=100_000_000, bytes_accessed=12_000_000, transcendentals=0
        ),
        name="on_grid",
    )(where, basis_z, layers, kap, fields)


def project_kernel(values, basis, plane_rows, out):
    along_x = lax.dot_general(
        plane_rows[...], values[...], (((0,), (0,)), ((), ())),
        precision=highest, preferred_element_type=f32,
    )
    full = lax.dot_general(
        along_x, basis[...], (((1,), (0,)), ((), ())),
        precision=highest, preferred_element_type=f32,
    )
    for y in range(4):
        for z in range(4):
            at = y * 64 + z * 16
            for h in range(2):
                out[z * 2 + h, pl.ds(y * 16, 16)] = full[at : at + 16, h * 128 : (h + 1) * 128]


def project(values, basis, plane_rows):
    return pl.pallas_call(
        project_kernel,
        out_shape=jax.ShapeDtypeStruct((8, 64, 128), f32),
        in_specs=[VMEM, VMEM, VMEM],
        out_specs=VMEM,
        compiler_params=params(48),
        cost_estimate=pl.CostEstimate(
            flops=6 * 2 * 256 * 128 * 1280, bytes_accessed=2_000_000, transcendentals=0
        ),
        name="project",
    )(values, basis, plane_rows)


def exchanged(values, axes):
    return lax.all_to_all(values, axes, split_axis=0, concat_axis=0, tiled=True)


def per_device(coefficients, first_axis_basis, basis_y, basis_z, conductivity, pressure):
    gx = lax.axis_index(GX)
    zh = lax.axis_index("zh")
    where = jnp.stack([gx, zh, lax.axis_index("zl")]).astype(jnp.int32)
    swap = [(0, 1), (1, 0)]

    flat = coefficients.reshape(DIRECTIONS * MODES_Z, 2, MODES)
    spread = jnp.broadcast_to(flat.reshape(4, 1, 8, 2, MODES), (4, 4, 8, 2, MODES))
    gathered = exchanged(spread.reshape(128, 2, MODES), GX)

    strip = lax.ppermute(pack(where, conductivity, pressure, basis_y), "zh", [(0, 1), (1, 0)])
    both = jnp.stack([conductivity, pressure])
    heads = jnp.concatenate([both[:, :, :HALO], strip[None, :DEPTH, :HALO]])
    tails = jnp.concatenate([both[:, :, -HALO:], strip[None, :DEPTH, -HALO:]])
    upper = lax.ppermute(heads, GX, [(i + 1, i) for i in range(127)])
    lower = lax.ppermute(tails, GX, [(i, i + 1) for i in range(127)])
    message = expand(where, gathered.reshape(MODES, MODES), basis_y, strip, first_axis_basis)
    message, upper, lower = lax.optimization_barrier((message, upper, lower))
    fields, plane_rows = statics(
        where, conductivity, pressure, upper, lower, strip, first_axis_basis
    )
    layers = exchanged(message, PLANE)
    modes = on_grid(where, basis_z, layers, conductivity, fields)
    columns = exchanged(modes, PLANE)
    shares = project(columns.reshape(4 * BLOCK, COLS), basis_y, plane_rows)
    summed = jnp.sum(exchanged(shares, RING), axis=0)
    result = exchanged(summed.reshape(32, 2, 128), PLANE)
    own = lax.dynamic_slice_in_dim(coefficients, zh * 128, 128, 3)
    return result.reshape(DIRECTIONS, MODES_Z, 2, 128) + own


def solution(mesh):
    split = Mesh(mesh.devices.reshape(SIZES), AXES)
    return jax.shard_map(
        per_device,
        mesh=split,
        in_specs=(
            P(None, None, GX, None),
            P(),
            P("zh", None),
            P(),
            P(None, GX, "zh"),
            P(None, GX, "zh"),
        ),
        out_specs=P(None, None, GX, "zh"),
        check_vma=False,
    )
```

```python
import jax
import jax.numpy as jnp
from jax import lax
from jax.experimental import pallas as pl
from jax.experimental.pallas import tpu as pltpu
from jax.sharding import Mesh, PartitionSpec as P

step_size = 0.05
highest = lax.Precision.HIGHEST
f32 = jnp.float32

AXES = ("y", "zl", "x", "core", "zh")
SIZES = (4, 4, 4, 2, 2)
GX = ("y", "zl", "x", "core")
PLANE = ("y", "x", "core")
RING = ("zl", "zh")

DIRECTIONS, MODES_Z, DEPTH = 2, 16, 32
ROWS, COLS = 32, 128
HALO = 4
EXT_ROWS = ROWS + 2 * HALO
EXT_COLS = 2 * COLS
STRIP = 8
GROUPS = EXT_ROWS // STRIP
PER_STEP = 16
LAYER_STEP = 4
STATIC_STEP = 8
STATIC_PARTS = 4
MODES = 256
FIELDS = 14
BLOCK = 8 * ROWS
VMEM = pl.BlockSpec(memory_space=pltpu.VMEM)
SMEM = pl.BlockSpec(memory_space=pltpu.SMEM)
HBM = pl.BlockSpec(memory_space=pltpu.HBM)


def place_in_grid():
    zl = lax.axis_index("zl")
    plane = lax.axis_index("x") * 2 + lax.axis_index("core")
    return (lax.axis_index("y") * 4 + zl) * 8 + plane, lax.axis_index("zh"), zl


def params(mib):
    return pltpu.CompilerParams(vmem_limit_bytes=mib * 1024 * 1024)


def strip_shift(zh, lane):
    return lax.rem(120 * zh + 2 * COLS - lane, COLS)


def columns_on(c, h, last):
    c, h = pltpu.roll(c, COLS - 1, 1), pltpu.roll(h, COLS - 1, 1)
    return jnp.where(last, h, c), jnp.where(last, c, h)


def pack_kernel(coefs, kap, prs, basis, spread, out):
    _, zh, _ = place_in_grid()
    for y in range(4):
        for part in range(4):
            values = coefs[pl.ds(8 * y, 8), part // 2, pl.ds(COLS * (part % 2), COLS)]
            for zl in range(4):
                spread[pl.ds((y * 4 + zl) * 32 + part, 8, stride=4), :] = values
    lane = lax.broadcasted_iota(jnp.int32, (STRIP, COLS), 1)

    def body(i, carry):
        for j in range(LAYER_STEP):
            z = i * LAYER_STEP + j
            packed = jnp.zeros((STRIP, COLS), f32)
            for f, ref in enumerate((kap, prs)):
                for g in range(ROWS // 8):
                    first = f * ROWS + 8 * g
                    moved = pltpu.roll(
                        ref[z, pl.ds(8 * g, 8)], lax.rem(first + 8 * (1 - zh), COLS), 1
                    )
                    packed = jnp.where((lane >= first) & (lane < first + 8), moved, packed)
            out[z] = packed
        return carry

    lax.fori_loop(0, DEPTH // LAYER_STEP, body, 0)
    edge = jnp.where(zh == 0, basis[COLS - STRIP :], basis[:STRIP])
    for part in range(2):
        out[DEPTH + part] = edge[:, COLS * part : COLS * (part + 1)]


def pack(coefs, kap, prs, basis):
    return pl.pallas_call(
        pack_kernel,
        out_shape=(
            jax.ShapeDtypeStruct((512, COLS), f32),
            jax.ShapeDtypeStruct((DEPTH + 2, STRIP, COLS), f32),
        ),
        in_specs=[VMEM] * 4,
        out_specs=(VMEM, VMEM),
        compiler_params=params(61),
        cost_estimate=pl.CostEstimate(
            flops=2_000_000, bytes_accessed=100_000_000, transcendentals=0
        ),
        name="pack",
    )(coefs, kap, prs, basis)


def expand_kernel(coefs, basis, beside, first_basis, out, wide, blocks, sems):
    _, _, zl = place_in_grid()
    copies = []
    for y in range(4):
        start = pl.multiple_of((y * 4 + zl) * BLOCK, BLOCK)
        below = pl.multiple_of(jnp.maximum(start - 8, 0), 8)
        above = pl.multiple_of(jnp.minimum(start + BLOCK, 4096 - 8), 8)
        for part, (src, size, dst) in enumerate(
            ((below, 8, 0), (start, BLOCK, 8), (above, 8, BLOCK + 8))
        ):
            copies.append(
                pltpu.make_async_copy(
                    first_basis.at[pl.ds(src, size)],
                    blocks.at[y, pl.ds(dst, size)],
                    sems.at[y, part],
                )
            )
    for copy in copies:
        copy.start()
    wide[pl.ds(0, COLS)] = basis[...]
    for part in range(2):
        wide[pl.ds(COLS, STRIP), pl.ds(COLS * part, COLS)] = beside[DEPTH + part]
    wide[pl.ds(COLS + STRIP, COLS - STRIP)] = jnp.zeros((COLS - STRIP, MODES), f32)
    modes = jnp.concatenate(
        [coefs[pl.ds(part, MODES, stride=2), :] for part in range(2)], axis=1
    )
    columns = lax.dot_general(
        modes, wide[...], (((1,), (1,)), ((), ())),
        precision=highest, preferred_element_type=f32,
    )
    lane = lax.broadcasted_iota(jnp.int32, (STRIP, COLS), 1)
    low = lax.broadcasted_iota(jnp.int32, (STRIP, EXT_COLS), 0) < HALO
    for copy in copies:
        copy.wait()
    for y in range(4):
        full = lax.dot_general(
            blocks[y], columns, (((1,), (0,)), ((), ())),
            precision=highest, preferred_element_type=f32,
        )
        for k in range(8):
            own = full[8 + ROWS * k : 8 + ROWS * (k + 1)]
            above = full[8 + ROWS * (k + 1) : 16 + ROWS * (k + 1)]
            below = full[ROWS * k : ROWS * k + 8]
            ends = jnp.where(low, above, below)
            q = y * 8 + k
            out[q, pl.ds(0, ROWS)] = own[:, :COLS]
            out[q, pl.ds(ROWS, 8)] = ends[:, :COLS]
            packed = own[:8, COLS:]
            for g in range(1, GROUPS):
                tile = (own[8 * g : 8 * g + 8] if g < ROWS // 8 else ends)[:, COLS:]
                packed = jnp.where(lane < 8 * g, packed, pltpu.roll(tile, 8 * g, 1))
            out[q, pl.ds(EXT_ROWS, STRIP)] = packed


def expand(coefs, basis, beside, first_basis):
    return pl.pallas_call(
        expand_kernel,
        out_shape=jax.ShapeDtypeStruct((32, EXT_ROWS + STRIP, COLS), f32),
        in_specs=[VMEM, VMEM, VMEM, HBM],
        out_specs=VMEM,
        scratch_shapes=[
            pltpu.VMEM((EXT_COLS, MODES), f32),
            pltpu.VMEM((4, BLOCK + 16, MODES), f32),
            pltpu.SemaphoreType.DMA((4, 3)),
        ],
        compiler_params=params(61),
        cost_estimate=pl.CostEstimate(
            flops=6 * 2 * 256 * 256 * 1344, bytes_accessed=40_000_000, transcendentals=0
        ),
        name="expand",
    )(coefs, basis, beside, first_basis)


def statics_kernel(
    kap, prs, upper, lower, strip, first_basis, out, plane_rows,
    built, pp, ph, held, sems, row_sems,
):
    kk, kh, pxc, pxh, pyc, pyh, pzc, pzh, exc, exh, eyc, eyh, ezc, ezh = (
        built.at[n] for n in range(FIELDS)
    )
    gx, zh, zl = place_in_grid()
    half = 0.5 * step_size * step_size
    row_copies = [
        pltpu.make_async_copy(
            first_basis.at[pl.ds(pl.multiple_of((y * 4 + zl) * BLOCK, BLOCK), BLOCK)],
            held.at[pl.ds(y * BLOCK, BLOCK)],
            row_sems.at[y],
        )
        for y in range(4)
    ]
    for copy in row_copies:
        copy.start()

    def place(i, carry):
        for j in range(STATIC_STEP):
            z = i * STATIC_STEP + j
            packed = strip[z]
            for f, (src, dst, far) in enumerate(((kap, kk, kh), (prs, pp, ph))):
                low, high = pl.ds(0, HALO), pl.ds(HALO + ROWS, HALO)
                dst[z, pl.ds(HALO, ROWS)] = src[z]
                dst[z, low] = lower[f, z]
                dst[z, high] = upper[f, z]
                for g in range(ROWS // 8):
                    far[z, pl.ds(HALO + 8 * g, 8)] = pltpu.roll(
                        packed, strip_shift(zh, f * ROWS + 8 * g), 1
                    )
                corners = jnp.concatenate([lower[2, z], upper[2, z]], axis=0)
                far[z, low] = pltpu.roll(corners, strip_shift(zh, (f + 1) * ROWS - 8), 1)[:HALO]
                far[z, high] = pltpu.roll(corners, strip_shift(zh, f * ROWS), 1)[HALO:]
        return carry

    lax.fori_loop(0, DEPTH // STATIC_STEP, place, 0)

    lane = lax.broadcasted_iota(jnp.int32, (8, COLS), 1)
    row = lax.broadcasted_iota(jnp.int32, (8, COLS), 0)
    last = lane == COLS - 1
    mask_c = jnp.where(last & (zh == 1), 0.0, 1.0).astype(f32)
    mask_h = jnp.where(last & (zh == 0), 0.0, 1.0).astype(f32)
    lowest, highest_row = jnp.where(gx == 0, HALO - 1, -1), jnp.where(gx == 127, HALO + ROWS - 1, -1)

    copies = []
    span = DEPTH // STATIC_PARTS
    for part in range(STATIC_PARTS):
        begin, end = part * span // STATIC_STEP, (part + 1) * span // STATIC_STEP
        for start in (0, 8, 16, 24, 31):
            at, up = pl.ds(start, 8), pl.ds(start + 1, 8)
            here = row + start
            mask_x = jnp.where((here == lowest) | (here == highest_row), 0.0, 1.0).astype(f32)

            def along_x(i, carry, at=at, up=up, mask_x=mask_x):
                for j in range(STATIC_STEP):
                    z = i * STATIC_STEP + j
                    exc[z, at] = (half * mask_x) * (kk[z, at] + kk[z, up])
                    exh[z, at] = (half * mask_x) * (kh[z, at] + kh[z, up])
                    pxc[z, at] = (0.5 * mask_x) * (pp[z, up] - pp[z, at])
                    pxh[z, at] = (0.5 * mask_x) * (ph[z, up] - ph[z, at])
                return carry

            lax.fori_loop(begin, end, along_x, 0)

        for start in (0, 8, 16, 24, 32):
            at = pl.ds(start, 8)

            def along_yz(i, carry, at=at):
                for j in range(STATIC_STEP):
                    z = i * STATIC_STEP + j
                    later = jnp.minimum(z + 1, DEPTH - 1)
                    inside = jnp.where(z < DEPTH - 1, 1.0, 0.0).astype(f32)
                    c, h, p, q = kk[z, at], kh[z, at], pp[z, at], ph[z, at]
                    cn, hn = columns_on(c, h, last)
                    pn, qn = columns_on(p, q, last)
                    eyc[z, at] = (half * mask_c) * (c + cn)
                    eyh[z, at] = (half * mask_h) * (h + hn)
                    pyc[z, at] = (0.5 * mask_c) * (pn - p)
                    pyh[z, at] = (0.5 * mask_h) * (qn - q)
                    ezc[z, at] = (half * inside) * (c + kk[later, at])
                    ezh[z, at] = (half * inside) * (h + kh[later, at])
                    pzc[z, at] = (0.5 * inside) * (pp[later, at] - p)
                    pzh[z, at] = (0.5 * inside) * (ph[later, at] - q)
                return carry

            lax.fori_loop(begin, end, along_yz, 0)

        copies.append(
            pltpu.make_async_copy(
                built.at[:, pl.ds(part * span, span)], out.at[:, pl.ds(part * span, span)], sems.at[part]
            )
        )
        copies[-1].start()
    for copy in row_copies:
        copy.wait()
    copies.append(pltpu.make_async_copy(held, plane_rows, row_sems.at[4]))
    copies[-1].start()
    for copy in copies:
        copy.wait()


def statics(kap, prs, upper, lower, strip, first_basis):
    field = (DEPTH, EXT_ROWS, COLS)
    return pl.pallas_call(
        statics_kernel,
        out_shape=(
            jax.ShapeDtypeStruct((FIELDS,) + field, f32),
            jax.ShapeDtypeStruct((4 * BLOCK, MODES), f32),
        ),
        in_specs=[VMEM] * 5 + [HBM],
        out_specs=(HBM, HBM),
        scratch_shapes=[
            pltpu.VMEM((FIELDS,) + field, f32),
            pltpu.VMEM(field, f32),
            pltpu.VMEM(field, f32),
            pltpu.VMEM((4 * BLOCK, MODES), f32),
            pltpu.SemaphoreType.DMA((STATIC_PARTS,)),
            pltpu.SemaphoreType.DMA((5,)),
        ],
        compiler_params=params(52),
        cost_estimate=pl.CostEstimate(
            flops=20_000_000, bytes_accessed=150_000_000, transcendentals=0
        ),
        name="statics",
    )(kap, prs, upper, lower, strip, first_basis)


def grid_kernel(basis_z, layers, kap, fields, out, built, uc, uh, vc, vh, sens, sems):
    kk, kh, pxc, pxh, pyc, pyh, pzc, pzh, exc, exh, eyc, eyh, ezc, ezh = (
        built.at[n] for n in range(FIELDS)
    )
    copies = [
        pltpu.make_async_copy(
            fields.at[pl.ds(first, size)], built.at[pl.ds(first, size)], sems.at[n]
        )
        for n, (first, size) in enumerate(((0, 2), (2, 6), (8, 6)))
    ]
    for copy in copies:
        copy.start()
    copies[0].wait()
    _, zh, _ = place_in_grid()
    lane = lax.broadcasted_iota(jnp.int32, (8, COLS), 1)
    first, last = lane == 0, lane == COLS - 1
    tiles = (EXT_ROWS + STRIP) // 8

    def layers_of(i, carry):
        for d in range(DIRECTIONS):
            totals = [[None] * tiles for _ in range(LAYER_STEP)]
            for c in range(MODES_Z):
                parts = [layers[d * MODES_Z + c, pl.ds(8 * t, 8)] for t in range(tiles)]
                for j in range(LAYER_STEP):
                    weight = basis_z[i * LAYER_STEP + j, c]
                    for t in range(tiles):
                        term = weight * parts[t]
                        totals[j][t] = term if c == 0 else totals[j][t] + term
            for j in range(LAYER_STEP):
                z = i * LAYER_STEP + j
                packed = totals[j][tiles - 1]
                for g in range(GROUPS):
                    tile = pltpu.roll(packed, strip_shift(zh, 8 * g), 1)
                    if g < ROWS // 8:
                        at = pl.ds(HALO + 8 * g, 8)
                        uc[d, z, at] = kk[z, at] * totals[j][g]
                        uh[d, z, at] = kh[z, at] * tile
                    else:
                        low, high = pl.ds(0, HALO), pl.ds(HALO + ROWS, HALO)
                        uc[d, z, low] = kk[z, low] * totals[j][g][HALO:]
                        uh[d, z, low] = kh[z, low] * tile[HALO:]
                        uc[d, z, high] = kk[z, high] * totals[j][g][:HALO]
                        uh[d, z, high] = kh[z, high] * tile[:HALO]
        return carry

    lax.fori_loop(0, DEPTH // LAYER_STEP, layers_of, 0)

    def columns_back(c, h):
        c, h = pltpu.roll(c, 1, 1), pltpu.roll(h, 1, 1)
        return jnp.where(first, h, c), jnp.where(first, c, h)

    zero = jnp.zeros((8, COLS), f32)

    def sweep(starts, source, target, coeffs, join, scale):
        (src_c, src_h), (dst_c, dst_h) = source, target
        (axc, axh), (ayc, ayh), (azc, azh) = coeffs
        for start in starts:
            at, up, down = pl.ds(start, 8), pl.ds(start + 1, 8), pl.ds(start - 1, 8)

            def body(i, carry, at=at, up=up, down=down):
                carry = list(carry)
                for j in range(PER_STEP):
                    z = i * PER_STEP + j
                    later = jnp.minimum(z + 1, DEPTH - 1)
                    nxc, nxh, bxc, bxh = axc[z, at], axh[z, at], axc[z, down], axh[z, down]
                    nyc, nyh, nzc, nzh = ayc[z, at], ayh[z, at], azc[z, at], azh[z, at]
                    for d in range(DIRECTIONS):
                        c, h, fzc, fzh = carry[4 * d : 4 * d + 4]
                        cz, hz = src_c[d, later, at], src_h[d, later, at]
                        cy, hy = columns_on(c, h, last)
                        fyc, fyh = join(cy, c) * nyc, join(hy, h) * nyh
                        byc, byh = columns_back(fyc, fyh)
                        gzc, gzh = join(cz, c) * nzc, join(hz, h) * nzh
                        xc = join(src_c[d, z, up], c) * nxc - join(c, src_c[d, z, down]) * bxc
                        xh = join(src_h[d, z, up], h) * nxh - join(h, src_h[d, z, down]) * bxh
                        total_c = xc + (fyc - byc) + (gzc - fzc)
                        total_h = xh + (fyh - byh) + (gzh - fzh)
                        if scale is not None:
                            total_c = scale * c + total_c
                            total_h = scale * h + total_h
                        dst_c[d, z, at] = total_c
                        dst_h[d, z, at] = total_h
                        carry[4 * d : 4 * d + 4] = [cz, hz, gzc, gzh]
                return tuple(carry)

            begin = []
            for d in range(DIRECTIONS):
                begin += [src_c[d, 0, at], src_h[d, 0, at], zero, zero]
            lax.fori_loop(0, DEPTH // PER_STEP, body, tuple(begin))

    def plus(a, b):
        return a + b

    def minus(a, b):
        return a - b

    u, v = (uc, uh), (vc, vh)
    ps = ((pxc, pxh), (pyc, pyh), (pzc, pzh))
    es = ((exc, exh), (eyc, eyh), (ezc, ezh))
    copies[1].wait()
    sweep((1, 9, 17, 25, 31), u, v, ps, plus, None)
    copies[2].wait()
    sweep((2, 10, 18, 26, 30), v, u, es, minus, 2.0 * step_size)
    sweep((3, 11, 19, 27, 29), u, v, es, minus, 2.0 * step_size)

    for start in (4, 12, 20, 28):
        at, up, down = pl.ds(start, 8), pl.ds(start + 1, 8), pl.ds(start - 1, 8)
        own = pl.ds(start - HALO, 8)

        def couple(i, carry, at=at, up=up, down=down, own=own):
            carry = list(carry)
            for j in range(PER_STEP):
                z = i * PER_STEP + j
                later = jnp.minimum(z + 1, DEPTH - 1)
                nxc, bxc, nyc, nyh, nzc = (
                    pxc[z, at], pxc[z, down], pyc[z, at], pyh[z, at], pzc[z, at]
                )
                weight = -kap[z, own]
                for d in range(DIRECTIONS):
                    c, fzc = carry[2 * d : 2 * d + 2]
                    h = vh[d, z, at]
                    cz = vc[d, later, at]
                    cy, hy = columns_on(c, h, last)
                    fyc, fyh = (cy - c) * nyc, (hy - h) * nyh
                    byc, _ = columns_back(fyc, fyh)
                    gzc = (cz - c) * nzc
                    xc = (vc[d, z, up] - c) * nxc + (c - vc[d, z, down]) * bxc
                    sens[d, z, own] = weight * (xc + (fyc + byc) + (gzc + fzc))
                    carry[2 * d : 2 * d + 2] = [cz, gzc]
            return tuple(carry)

        begin = []
        for d in range(DIRECTIONS):
            begin += [vc[d, 0, at], zero]
        lax.fori_loop(0, DEPTH // PER_STEP, couple, tuple(begin))

    def modes_of(c, carry):
        for d in range(DIRECTIONS):
            total = basis_z[0, c] * sens[d, 0]
            for z in range(1, DEPTH):
                total = total + basis_z[z, c] * sens[d, z]
            out[d * MODES_Z + c] = total
        return carry

    lax.fori_loop(0, MODES_Z, modes_of, 0)


def on_grid(basis_z, layers, kap, fields):
    wide = (DIRECTIONS, DEPTH, EXT_ROWS, COLS)
    return pl.pallas_call(
        grid_kernel,
        out_shape=jax.ShapeDtypeStruct((DIRECTIONS * MODES_Z, ROWS, COLS), f32),
        in_specs=[SMEM, VMEM, VMEM, HBM],
        out_specs=VMEM,
        scratch_shapes=[pltpu.VMEM((FIELDS, DEPTH, EXT_ROWS, COLS), f32)]
        + [pltpu.VMEM(wide, f32) for _ in range(4)]
        + [
            pltpu.VMEM((DIRECTIONS, DEPTH, ROWS, COLS), f32),
            pltpu.SemaphoreType.DMA((3,)),
        ],
        compiler_params=params(52),
        cost_estimate=pl.CostEstimate(
            flops=100_000_000, bytes_accessed=12_000_000, transcendentals=0
        ),
        name="on_grid",
    )(basis_z, layers, kap, fields)


def project_kernel(values, basis, plane_rows, out):
    along_x = lax.dot_general(
        plane_rows[...], values[...], (((0,), (0,)), ((), ())),
        precision=highest, preferred_element_type=f32,
    )
    full = lax.dot_general(
        along_x, basis[...], (((1,), (0,)), ((), ())),
        precision=highest, preferred_element_type=f32,
    )
    for y in range(4):
        for z in range(4):
            at = y * 64 + z * 16
            for h in range(2):
                out[z * 2 + h, pl.ds(y * 16, 16)] = full[at : at + 16, h * 128 : (h + 1) * 128]


def project(values, basis, plane_rows):
    return pl.pallas_call(
        project_kernel,
        out_shape=jax.ShapeDtypeStruct((8, 64, 128), f32),
        in_specs=[VMEM, VMEM, VMEM],
        out_specs=VMEM,
        compiler_params=params(48),
        cost_estimate=pl.CostEstimate(
            flops=6 * 2 * 256 * 128 * 1280, bytes_accessed=2_000_000, transcendentals=0
        ),
        name="project",
    )(values, basis, plane_rows)


def exchanged(values, axes):
    return lax.all_to_all(values, axes, split_axis=0, concat_axis=0, tiled=True)


def per_device(coefficients, first_axis_basis, basis_y, basis_z, conductivity, pressure):
    zh = lax.axis_index("zh")
    flat = coefficients.reshape(DIRECTIONS * MODES_Z, 2, MODES)
    spread, strip = pack(flat, conductivity, pressure, basis_y)
    gathered = exchanged(spread.reshape(128, 4, COLS), GX)
    strip = lax.ppermute(strip, "zh", [(0, 1), (1, 0)])
    both = jnp.stack([conductivity, pressure])
    heads = jnp.concatenate([both[:, :, :HALO], strip[None, :DEPTH, :HALO]])
    tails = jnp.concatenate([both[:, :, -HALO:], strip[None, :DEPTH, -HALO:]])
    upper = lax.ppermute(heads, GX, [(i + 1, i) for i in range(127)])
    lower = lax.ppermute(tails, GX, [(i, i + 1) for i in range(127)])
    message = expand(gathered.reshape(512, COLS), basis_y, strip, first_axis_basis)
    message, upper, lower = lax.optimization_barrier((message, upper, lower))
    fields, plane_rows = statics(conductivity, pressure, upper, lower, strip, first_axis_basis)
    layers = exchanged(message, PLANE)
    modes = on_grid(basis_z, layers, conductivity, fields)
    columns = exchanged(modes, PLANE)
    shares = project(columns.reshape(4 * BLOCK, COLS), basis_y, plane_rows)
    summed = jnp.sum(exchanged(shares, RING), axis=0)
    result = exchanged(summed.reshape(32, 2, 128), PLANE)
    own = lax.dynamic_slice_in_dim(coefficients, zh * 128, 128, 3)
    return result.reshape(DIRECTIONS, MODES_Z, 2, 128) + own


def solution(mesh):
    split = Mesh(mesh.devices.reshape(SIZES), AXES)
    return jax.shard_map(
        per_device,
        mesh=split,
        in_specs=(
            P(None, None, GX, None),
            P(),
            P("zh", None),
            P(),
            P(None, GX, "zh"),
            P(None, GX, "zh"),
        ),
        out_specs=P(None, None, GX, "zh"),
        check_vma=False,
    )
```

```python
import jax
import jax.numpy as jnp
from jax import lax
from jax.experimental import pallas as pl
from jax.experimental.pallas import tpu as pltpu
from jax.sharding import Mesh, PartitionSpec as P

step_size = 0.05
highest = lax.Precision.HIGHEST
f32 = jnp.float32

AXES = ("y", "zl", "x", "core", "zh")
SIZES = (4, 4, 4, 2, 2)
GX = ("y", "zl", "x", "core")
PLANE = ("y", "x", "core")
RING = ("zl", "zh")

DIRECTIONS, MODES_Z, DEPTH = 2, 16, 32
ROWS, COLS = 32, 128
HALO = 4
EXT_ROWS = ROWS + 2 * HALO
EXT_COLS = 2 * COLS
STRIP = 8
GROUPS = EXT_ROWS // STRIP
PER_STEP = 16
LAYER_STEP = 4
STATIC_STEP = 8
STATIC_PARTS = 4
MODES = 256
FIELDS = 14
BLOCK = 8 * ROWS
VMEM = pl.BlockSpec(memory_space=pltpu.VMEM)
SMEM = pl.BlockSpec(memory_space=pltpu.SMEM)
HBM = pl.BlockSpec(memory_space=pltpu.HBM)


def place_in_grid():
    zl = lax.axis_index("zl")
    plane = lax.axis_index("x") * 2 + lax.axis_index("core")
    return (lax.axis_index("y") * 4 + zl) * 8 + plane, lax.axis_index("zh"), zl


def params(mib):
    return pltpu.CompilerParams(vmem_limit_bytes=mib * 1024 * 1024)


def strip_shift(zh, lane):
    return lax.rem(120 * zh + 2 * COLS - lane, COLS)


def columns_on(c, h, last):
    c, h = pltpu.roll(c, COLS - 1, 1), pltpu.roll(h, COLS - 1, 1)
    return jnp.where(last, h, c), jnp.where(last, c, h)


def pack_kernel(coefs, kap, prs, basis, spread, out):
    _, zh, _ = place_in_grid()
    for y in range(4):
        for part in range(4):
            values = coefs[pl.ds(8 * y, 8), part // 2, pl.ds(COLS * (part % 2), COLS)]
            for zl in range(4):
                spread[pl.ds((y * 4 + zl) * 32 + part, 8, stride=4), :] = values
    lane = lax.broadcasted_iota(jnp.int32, (STRIP, COLS), 1)

    def body(i, carry):
        for j in range(LAYER_STEP):
            z = i * LAYER_STEP + j
            packed = jnp.zeros((STRIP, COLS), f32)
            for f, ref in enumerate((kap, prs)):
                for g in range(ROWS // 8):
                    first = f * ROWS + 8 * g
                    moved = pltpu.roll(
                        ref[z, pl.ds(8 * g, 8)], lax.rem(first + 8 * (1 - zh), COLS), 1
                    )
                    packed = jnp.where((lane >= first) & (lane < first + 8), moved, packed)
            out[z] = packed
        return carry

    lax.fori_loop(0, DEPTH // LAYER_STEP, body, 0)
    edge = jnp.where(zh == 0, basis[COLS - STRIP :], basis[:STRIP])
    for part in range(2):
        out[DEPTH + part] = edge[:, COLS * part : COLS * (part + 1)]


def pack(coefs, kap, prs, basis):
    return pl.pallas_call(
        pack_kernel,
        out_shape=(
            jax.ShapeDtypeStruct((512, COLS), f32),
            jax.ShapeDtypeStruct((DEPTH + 2, STRIP, COLS), f32),
        ),
        in_specs=[VMEM] * 4,
        out_specs=(VMEM, VMEM),
        compiler_params=params(61),
        cost_estimate=pl.CostEstimate(
            flops=2_000_000, bytes_accessed=100_000_000, transcendentals=0
        ),
        name="pack",
    )(coefs, kap, prs, basis)


def expand_kernel(coefs, basis, beside, first_basis, out, wide, blocks, sems):
    _, _, zl = place_in_grid()
    copies = []
    for y in range(4):
        start = pl.multiple_of((y * 4 + zl) * BLOCK, BLOCK)
        below = pl.multiple_of(jnp.maximum(start - 8, 0), 8)
        above = pl.multiple_of(jnp.minimum(start + BLOCK, 4096 - 8), 8)
        for part, (src, size, dst) in enumerate(
            ((below, 8, 0), (start, BLOCK, 8), (above, 8, BLOCK + 8))
        ):
            copies.append(
                pltpu.make_async_copy(
                    first_basis.at[pl.ds(src, size)],
                    blocks.at[y, pl.ds(dst, size)],
                    sems.at[y, part],
                )
            )
    for copy in copies:
        copy.start()
    wide[pl.ds(0, COLS)] = basis[...]
    for part in range(2):
        wide[pl.ds(COLS, STRIP), pl.ds(COLS * part, COLS)] = beside[DEPTH + part]
    wide[pl.ds(COLS + STRIP, COLS - STRIP)] = jnp.zeros((COLS - STRIP, MODES), f32)
    modes = jnp.concatenate(
        [coefs[pl.ds(part, MODES, stride=2), :] for part in range(2)], axis=1
    )
    columns = lax.dot_general(
        modes, wide[...], (((1,), (1,)), ((), ())),
        precision=highest, preferred_element_type=f32,
    )
    lane = lax.broadcasted_iota(jnp.int32, (STRIP, COLS), 1)
    low = lax.broadcasted_iota(jnp.int32, (STRIP, EXT_COLS), 0) < HALO
    for copy in copies:
        copy.wait()
    for y in range(4):
        full = lax.dot_general(
            blocks[y], columns, (((1,), (0,)), ((), ())),
            precision=highest, preferred_element_type=f32,
        )
        for k in range(8):
            own = full[8 + ROWS * k : 8 + ROWS * (k + 1)]
            above = full[8 + ROWS * (k + 1) : 16 + ROWS * (k + 1)]
            below = full[ROWS * k : ROWS * k + 8]
            ends = jnp.where(low, above, below)
            q = y * 8 + k
            out[q, pl.ds(0, ROWS)] = own[:, :COLS]
            out[q, pl.ds(ROWS, 8)] = ends[:, :COLS]
            packed = own[:8, COLS:]
            for g in range(1, GROUPS):
                tile = (own[8 * g : 8 * g + 8] if g < ROWS // 8 else ends)[:, COLS:]
                packed = jnp.where(lane < 8 * g, packed, pltpu.roll(tile, 8 * g, 1))
            out[q, pl.ds(EXT_ROWS, STRIP)] = packed


def expand(coefs, basis, beside, first_basis):
    return pl.pallas_call(
        expand_kernel,
        out_shape=jax.ShapeDtypeStruct((32, EXT_ROWS + STRIP, COLS), f32),
        in_specs=[VMEM, VMEM, VMEM, HBM],
        out_specs=VMEM,
        scratch_shapes=[
            pltpu.VMEM((EXT_COLS, MODES), f32),
            pltpu.VMEM((4, BLOCK + 16, MODES), f32),
            pltpu.SemaphoreType.DMA((4, 3)),
        ],
        compiler_params=params(61),
        cost_estimate=pl.CostEstimate(
            flops=6 * 2 * 256 * 256 * 1344, bytes_accessed=40_000_000, transcendentals=0
        ),
        name="expand",
    )(coefs, basis, beside, first_basis)


def statics_kernel(
    kap, prs, upper, lower, strip, first_basis, out, plane_rows,
    built, pp, ph, held, sems, row_sems,
):
    kk, kh, pxc, pxh, pyc, pyh, pzc, pzh, exc, exh, eyc, eyh, ezc, ezh = (
        built.at[n] for n in range(FIELDS)
    )
    gx, zh, zl = place_in_grid()
    half = 0.5 * step_size * step_size
    row_copies = [
        pltpu.make_async_copy(
            first_basis.at[pl.ds(pl.multiple_of((y * 4 + zl) * BLOCK, BLOCK), BLOCK)],
            held.at[pl.ds(y * BLOCK, BLOCK)],
            row_sems.at[y],
        )
        for y in range(4)
    ]
    for copy in row_copies:
        copy.start()

    def place(i, carry):
        for j in range(STATIC_STEP):
            z = i * STATIC_STEP + j
            packed = strip[z]
            for f, (src, dst, far) in enumerate(((kap, kk, kh), (prs, pp, ph))):
                low, high = pl.ds(0, HALO), pl.ds(HALO + ROWS, HALO)
                dst[z, pl.ds(HALO, ROWS)] = src[z]
                dst[z, low] = lower[f, z]
                dst[z, high] = upper[f, z]
                for g in range(ROWS // 8):
                    far[z, pl.ds(HALO + 8 * g, 8)] = pltpu.roll(
                        packed, strip_shift(zh, f * ROWS + 8 * g), 1
                    )
                corners = jnp.concatenate([lower[2, z], upper[2, z]], axis=0)
                far[z, low] = pltpu.roll(corners, strip_shift(zh, (f + 1) * ROWS - 8), 1)[:HALO]
                far[z, high] = pltpu.roll(corners, strip_shift(zh, f * ROWS), 1)[HALO:]
        return carry

    lax.fori_loop(0, DEPTH // STATIC_STEP, place, 0)

    lane = lax.broadcasted_iota(jnp.int32, (8, COLS), 1)
    row = lax.broadcasted_iota(jnp.int32, (8, COLS), 0)
    last = lane == COLS - 1
    mask_c = jnp.where(last & (zh == 1), 0.0, 1.0).astype(f32)
    mask_h = jnp.where(last & (zh == 0), 0.0, 1.0).astype(f32)
    lowest, highest_row = jnp.where(gx == 0, HALO - 1, -1), jnp.where(gx == 127, HALO + ROWS - 1, -1)

    copies = []
    span = DEPTH // STATIC_PARTS
    for part in range(STATIC_PARTS):
        begin, end = part * span // STATIC_STEP, (part + 1) * span // STATIC_STEP
        for start in (0, 8, 16, 24, 31):
            at, up = pl.ds(start, 8), pl.ds(start + 1, 8)
            here = row + start
            mask_x = jnp.where((here == lowest) | (here == highest_row), 0.0, 1.0).astype(f32)

            def along_x(i, carry, at=at, up=up, mask_x=mask_x):
                for j in range(STATIC_STEP):
                    z = i * STATIC_STEP + j
                    exc[z, at] = (half * mask_x) * (kk[z, at] + kk[z, up])
                    exh[z, at] = (half * mask_x) * (kh[z, at] + kh[z, up])
                    pxc[z, at] = (0.5 * mask_x) * (pp[z, up] - pp[z, at])
                    pxh[z, at] = (0.5 * mask_x) * (ph[z, up] - ph[z, at])
                return carry

            lax.fori_loop(begin, end, along_x, 0)

        for start in (0, 8, 16, 24, 32):
            at = pl.ds(start, 8)

            def along_yz(i, carry, at=at):
                for j in range(STATIC_STEP):
                    z = i * STATIC_STEP + j
                    later = jnp.minimum(z + 1, DEPTH - 1)
                    inside = jnp.where(z < DEPTH - 1, 1.0, 0.0).astype(f32)
                    c, h, p, q = kk[z, at], kh[z, at], pp[z, at], ph[z, at]
                    cn, hn = columns_on(c, h, last)
                    pn, qn = columns_on(p, q, last)
                    eyc[z, at] = (half * mask_c) * (c + cn)
                    eyh[z, at] = (half * mask_h) * (h + hn)
                    pyc[z, at] = (0.5 * mask_c) * (pn - p)
                    pyh[z, at] = (0.5 * mask_h) * (qn - q)
                    ezc[z, at] = (half * inside) * (c + kk[later, at])
                    ezh[z, at] = (half * inside) * (h + kh[later, at])
                    pzc[z, at] = (0.5 * inside) * (pp[later, at] - p)
                    pzh[z, at] = (0.5 * inside) * (ph[later, at] - q)
                return carry

            lax.fori_loop(begin, end, along_yz, 0)

        copies.append(
            pltpu.make_async_copy(
                built.at[:, pl.ds(part * span, span)], out.at[:, pl.ds(part * span, span)], sems.at[part]
            )
        )
        copies[-1].start()
    for copy in row_copies:
        copy.wait()
    copies.append(pltpu.make_async_copy(held, plane_rows, row_sems.at[4]))
    copies[-1].start()
    for copy in copies:
        copy.wait()


def statics(kap, prs, upper, lower, strip, first_basis):
    field = (DEPTH, EXT_ROWS, COLS)
    return pl.pallas_call(
        statics_kernel,
        out_shape=(
            jax.ShapeDtypeStruct((FIELDS,) + field, f32),
            jax.ShapeDtypeStruct((4 * BLOCK, MODES), f32),
        ),
        in_specs=[VMEM] * 5 + [HBM],
        out_specs=(HBM, HBM),
        scratch_shapes=[
            pltpu.VMEM((FIELDS,) + field, f32),
            pltpu.VMEM(field, f32),
            pltpu.VMEM(field, f32),
            pltpu.VMEM((4 * BLOCK, MODES), f32),
            pltpu.SemaphoreType.DMA((STATIC_PARTS,)),
            pltpu.SemaphoreType.DMA((5,)),
        ],
        compiler_params=params(52),
        cost_estimate=pl.CostEstimate(
            flops=20_000_000, bytes_accessed=150_000_000, transcendentals=0
        ),
        name="statics",
    )(kap, prs, upper, lower, strip, first_basis)


def grid_kernel(basis_z, layers, kap, fields, out, built, uc, uh, vc, vh, sens, sems):
    kk, kh, pxc, pxh, pyc, pyh, pzc, pzh, exc, exh, eyc, eyh, ezc, ezh = (
        built.at[n] for n in range(FIELDS)
    )
    copies = [
        pltpu.make_async_copy(
            fields.at[pl.ds(first, size)], built.at[pl.ds(first, size)], sems.at[n]
        )
        for n, (first, size) in enumerate(((0, 2), (2, 6), (8, 6)))
    ]
    for copy in copies:
        copy.start()
    copies[0].wait()
    _, zh, _ = place_in_grid()
    lane = lax.broadcasted_iota(jnp.int32, (8, COLS), 1)
    first, last = lane == 0, lane == COLS - 1
    tiles = (EXT_ROWS + STRIP) // 8

    def layers_of(i, carry):
        for d in range(DIRECTIONS):
            totals = [[None] * tiles for _ in range(LAYER_STEP)]
            for c in range(MODES_Z):
                parts = [layers[d * MODES_Z + c, pl.ds(8 * t, 8)] for t in range(tiles)]
                for j in range(LAYER_STEP):
                    weight = basis_z[i * LAYER_STEP + j, c]
                    for t in range(tiles):
                        term = weight * parts[t]
                        totals[j][t] = term if c == 0 else totals[j][t] + term
            for j in range(LAYER_STEP):
                z = i * LAYER_STEP + j
                packed = totals[j][tiles - 1]
                for g in range(GROUPS):
                    tile = pltpu.roll(packed, strip_shift(zh, 8 * g), 1)
                    if g < ROWS // 8:
                        at = pl.ds(HALO + 8 * g, 8)
                        uc[d, z, at] = kk[z, at] * totals[j][g]
                        uh[d, z, at] = kh[z, at] * tile
                    else:
                        low, high = pl.ds(0, HALO), pl.ds(HALO + ROWS, HALO)
                        uc[d, z, low] = kk[z, low] * totals[j][g][HALO:]
                        uh[d, z, low] = kh[z, low] * tile[HALO:]
                        uc[d, z, high] = kk[z, high] * totals[j][g][:HALO]
                        uh[d, z, high] = kh[z, high] * tile[:HALO]
        return carry

    lax.fori_loop(0, DEPTH // LAYER_STEP, layers_of, 0)

    def columns_back(c, h):
        c, h = pltpu.roll(c, 1, 1), pltpu.roll(h, 1, 1)
        return jnp.where(first, h, c), jnp.where(first, c, h)

    zero = jnp.zeros((8, COLS), f32)

    def sweep(starts, source, target, coeffs, join, scale):
        (src_c, src_h), (dst_c, dst_h) = source, target
        (axc, axh), (ayc, ayh), (azc, azh) = coeffs
        for start in starts:
            at, up, down = pl.ds(start, 8), pl.ds(start + 1, 8), pl.ds(start - 1, 8)

            def body(i, carry, at=at, up=up, down=down):
                carry = list(carry)
                for j in range(PER_STEP):
                    z = i * PER_STEP + j
                    later = jnp.minimum(z + 1, DEPTH - 1)
                    nxc, nxh, bxc, bxh = axc[z, at], axh[z, at], axc[z, down], axh[z, down]
                    nyc, nyh, nzc, nzh = ayc[z, at], ayh[z, at], azc[z, at], azh[z, at]
                    for d in range(DIRECTIONS):
                        c, h, fzc, fzh = carry[4 * d : 4 * d + 4]
                        cz, hz = src_c[d, later, at], src_h[d, later, at]
                        cy, hy = columns_on(c, h, last)
                        fyc, fyh = join(cy, c) * nyc, join(hy, h) * nyh
                        byc, byh = columns_back(fyc, fyh)
                        gzc, gzh = join(cz, c) * nzc, join(hz, h) * nzh
                        xc = join(src_c[d, z, up], c) * nxc - join(c, src_c[d, z, down]) * bxc
                        xh = join(src_h[d, z, up], h) * nxh - join(h, src_h[d, z, down]) * bxh
                        total_c = xc + (fyc - byc) + (gzc - fzc)
                        total_h = xh + (fyh - byh) + (gzh - fzh)
                        if scale is not None:
                            total_c = scale * c + total_c
                            total_h = scale * h + total_h
                        dst_c[d, z, at] = total_c
                        dst_h[d, z, at] = total_h
                        carry[4 * d : 4 * d + 4] = [cz, hz, gzc, gzh]
                return tuple(carry)

            begin = []
            for d in range(DIRECTIONS):
                begin += [src_c[d, 0, at], src_h[d, 0, at], zero, zero]
            lax.fori_loop(0, DEPTH // PER_STEP, body, tuple(begin))

    def plus(a, b):
        return a + b

    def minus(a, b):
        return a - b

    u, v = (uc, uh), (vc, vh)
    ps = ((pxc, pxh), (pyc, pyh), (pzc, pzh))
    es = ((exc, exh), (eyc, eyh), (ezc, ezh))
    copies[1].wait()
    sweep((1, 9, 17, 25, 31), u, v, ps, plus, None)
    copies[2].wait()
    sweep((2, 10, 18, 26, 30), v, u, es, minus, 2.0 * step_size)
    sweep((3, 11, 19, 27, 29), u, v, es, minus, 2.0 * step_size)

    for start in (4, 12, 20, 28):
        at, up, down = pl.ds(start, 8), pl.ds(start + 1, 8), pl.ds(start - 1, 8)
        own = pl.ds(start - HALO, 8)

        def couple(i, carry, at=at, up=up, down=down, own=own):
            carry = list(carry)
            for j in range(PER_STEP):
                z = i * PER_STEP + j
                later = jnp.minimum(z + 1, DEPTH - 1)
                nxc, bxc, nyc, nyh, nzc = (
                    pxc[z, at], pxc[z, down], pyc[z, at], pyh[z, at], pzc[z, at]
                )
                weight = -kap[z, own]
                for d in range(DIRECTIONS):
                    c, fzc = carry[2 * d : 2 * d + 2]
                    h = vh[d, z, at]
                    cz = vc[d, later, at]
                    cy, hy = columns_on(c, h, last)
                    fyc, fyh = (cy - c) * nyc, (hy - h) * nyh
                    byc, _ = columns_back(fyc, fyh)
                    gzc = (cz - c) * nzc
                    xc = (vc[d, z, up] - c) * nxc + (c - vc[d, z, down]) * bxc
                    sens[d, z, own] = weight * (xc + (fyc + byc) + (gzc + fzc))
                    carry[2 * d : 2 * d + 2] = [cz, gzc]
            return tuple(carry)

        begin = []
        for d in range(DIRECTIONS):
            begin += [vc[d, 0, at], zero]
        lax.fori_loop(0, DEPTH // PER_STEP, couple, tuple(begin))

    def modes_of(c, carry):
        for d in range(DIRECTIONS):
            total = basis_z[0, c] * sens[d, 0]
            for z in range(1, DEPTH):
                total = total + basis_z[z, c] * sens[d, z]
            out[d * MODES_Z + c] = total
        return carry

    lax.fori_loop(0, MODES_Z, modes_of, 0)


def on_grid(basis_z, layers, kap, fields):
    wide = (DIRECTIONS, DEPTH, EXT_ROWS, COLS)
    return pl.pallas_call(
        grid_kernel,
        out_shape=jax.ShapeDtypeStruct((DIRECTIONS * MODES_Z, ROWS, COLS), f32),
        in_specs=[SMEM, VMEM, VMEM, HBM],
        out_specs=VMEM,
        scratch_shapes=[pltpu.VMEM((FIELDS, DEPTH, EXT_ROWS, COLS), f32)]
        + [pltpu.VMEM(wide, f32) for _ in range(4)]
        + [
            pltpu.VMEM((DIRECTIONS, DEPTH, ROWS, COLS), f32),
            pltpu.SemaphoreType.DMA((3,)),
        ],
        compiler_params=params(52),
        cost_estimate=pl.CostEstimate(
            flops=100_000_000, bytes_accessed=12_000_000, transcendentals=0
        ),
        name="on_grid",
    )(basis_z, layers, kap, fields)


def project_kernel(values, basis, plane_rows, out):
    along_x = lax.dot_general(
        plane_rows[...], values[...], (((0,), (0,)), ((), ())),
        precision=highest, preferred_element_type=f32,
    )
    full = lax.dot_general(
        along_x, basis[...], (((1,), (0,)), ((), ())),
        precision=highest, preferred_element_type=f32,
    )
    for y in range(4):
        for z in range(4):
            at = y * 64 + z * 16
            for h in range(2):
                out[z * 2 + h, pl.ds(y * 16, 16)] = full[at : at + 16, h * 128 : (h + 1) * 128]


def project(values, basis, plane_rows):
    return pl.pallas_call(
        project_kernel,
        out_shape=jax.ShapeDtypeStruct((8, 64, 128), f32),
        in_specs=[VMEM, VMEM, VMEM],
        out_specs=VMEM,
        compiler_params=params(48),
        cost_estimate=pl.CostEstimate(
            flops=6 * 2 * 256 * 128 * 1280, bytes_accessed=2_000_000, transcendentals=0
        ),
        name="project",
    )(values, basis, plane_rows)


def exchanged(values, axes):
    return lax.all_to_all(values, axes, split_axis=0, concat_axis=0, tiled=True)


def per_device(coefficients, first_axis_basis, basis_y, basis_z, conductivity, pressure):
    zh = lax.axis_index("zh")
    flat = coefficients.reshape(DIRECTIONS * MODES_Z, 2, MODES)
    spread, strip = pack(flat, conductivity, pressure, basis_y)
    gathered = exchanged(spread.reshape(128, 4, COLS), GX)
    strip = lax.ppermute(strip, "zh", [(0, 1), (1, 0)])
    both = jnp.stack([conductivity, pressure])
    heads = jnp.concatenate([both[:, :, :HALO], strip[None, :DEPTH, :HALO]])
    tails = jnp.concatenate([both[:, :, -HALO:], strip[None, :DEPTH, -HALO:]])
    upper = lax.ppermute(heads, GX, [(i + 1, i) for i in range(127)])
    lower = lax.ppermute(tails, GX, [(i, i + 1) for i in range(127)])
    message = expand(gathered.reshape(512, COLS), basis_y, strip, first_axis_basis)
    fields, plane_rows = statics(conductivity, pressure, upper, lower, strip, first_axis_basis)
    layers = exchanged(message, PLANE)
    modes = on_grid(basis_z, layers, conductivity, fields)
    columns = exchanged(modes, PLANE)
    shares = project(columns.reshape(4 * BLOCK, COLS), basis_y, plane_rows)
    summed = jnp.sum(exchanged(shares, RING), axis=0)
    result = exchanged(summed.reshape(32, 2, 128), PLANE)
    own = lax.dynamic_slice_in_dim(coefficients, zh * 128, 128, 3)
    return result.reshape(DIRECTIONS, MODES_Z, 2, 128) + own


def solution(mesh):
    split = Mesh(mesh.devices.reshape(SIZES), AXES)
    return jax.shard_map(
        per_device,
        mesh=split,
        in_specs=(
            P(None, None, GX, None),
            P(),
            P("zh", None),
            P(),
            P(None, GX, "zh"),
            P(None, GX, "zh"),
        ),
        out_specs=P(None, None, GX, "zh"),
        check_vma=False,
    )
```
